32 devices in a mesh: fsdp: 2 (over x), ctx: 4 (over z), tp: 4 (over y, core).
Axes of the slice: x: 2, y: 2, z: 4, core: 2. Of those that a mesh axis runs over, the one named last changes fastest.
Arguments:
- inputs: bfloat16 [1024, 8, 1024], P('ctx', 'fsdp'), may hold values from -6 to 6
- cotangent: bfloat16 [1024, 8, 1024], P('ctx', 'fsdp'), may hold values from -6 to 6
- ln1_gain: bfloat16 [1024], P('fsdp'), may hold values from 0.5 to 1.5
- ln1_bias: bfloat16 [1024], P('fsdp'), may hold values from -4 to 4
- qkv_weight: bfloat16 [3, 1024, 1024], P(None, 'fsdp', 'tp'), may hold values from -0.25 to 0.25
- qv_bias: bfloat16 [2, 16, 64], P(None, 'tp', 'fsdp'), may hold values from -6 to 6
- proj_weight: bfloat16 [1024, 1024], P('tp', 'fsdp'), may hold values from -0.375 to 0.375
- proj_bias: bfloat16 [1024], P('fsdp'), may hold values from -4 to 4
- ln2_gain: bfloat16 [1024], P('fsdp'), may hold values from 0.5 to 1.5
- ln2_bias: bfloat16 [1024], P('fsdp'), may hold values from -4 to 4
- fc_weight: bfloat16 [1024, 4096], P('fsdp', 'tp'), may hold values from -0.1875 to 0.1875
- fc_bias: bfloat16 [64, 64], P('tp', 'fsdp'), may hold values from -6 to 6
- fc2_weight: bfloat16 [4096, 1024], P('tp', 'fsdp'), may hold values from -0.09375 to 0.09375
- fc2_bias: bfloat16 [1024], P('fsdp'), may hold values from -4 to 4
Outputs:
- output: bfloat16 [1024, 8, 1024], P(('ctx', 'tp'), 'fsdp')
- input_grad: bfloat16 [1024, 8, 1024], P(('ctx', 'tp'), 'fsdp')
- grad_ln1_gain: float32 [1024], P('fsdp')
- grad_ln1_bias: float32 [1024], P('fsdp')
- grad_qkv_weight: float32 [3, 1024, 1024], P(None, 'fsdp', 'tp')
- grad_qv_bias: float32 [2, 16, 64], P(None, 'tp', 'fsdp')
- grad_proj_weight: float32 [1024, 1024], P('tp', 'fsdp')
- grad_proj_bias: float32 [1024], P('fsdp')
- grad_ln2_gain: float32 [1024], P('fsdp')
- grad_ln2_bias: float32 [1024], P('fsdp')
- grad_fc_weight: float32 [1024, 4096], P('fsdp', 'tp')
- grad_fc_bias: float32 [64, 64], P('tp', 'fsdp')
- grad_fc2_weight: float32 [4096, 1024], P('tp', 'fsdp')
- grad_fc2_bias: float32 [1024], P('fsdp')
The draws below stay inside these ranges and needn't reach their ends.
All inputs are finite; a program needn't handle non-finite values.
Results may differ from the reference program's by a relative error of at most 0.015.
The reference program's roundings to bfloat16 on the way count: a program that leaves them out, or rounds other values in their place, can miss the bound.
Values may be sent and summed in bfloat16 or wider, within the bound.
No kernel may reach another device: no remote copies, remote signals or barrier semaphores. Data moves between devices by JAX's collectives and lax.ppermute only.
A program may use at most 256 MiB of HBM per device.

```python
import functools
import jax
import jax.numpy as jnp
from jax import lax

D = 1024
HEADS = 16
HD = 64
FF = 4096
BLOCK = 256
SEQ_LEN = 1024
SEQUENCES = 8


def shard_levels(key, extent, split, least, largest):
    level, own = 1.0, jax.random.fold_in(key, 6)
    for position, parts in split:
        steps = jnp.exp(jax.random.uniform(jax.random.fold_in(own, position), (parts,), jnp.float32, least / len(split), largest / len(split)))
        level = level * jnp.repeat(steps, extent[position] // parts).reshape([-1 if axis == position else 1 for axis in range(len(extent))])
    return level


def noise(own_key, shape, scale, most, shards=(), kind=jnp.bfloat16):
    factor_of = shard_levels(own_key, shape, shards, -0.22, 0.18) if shards else 1.0
    values = jax.random.normal(own_key, shape, jnp.float32) * scale * factor_of
    return jnp.minimum(jnp.maximum(values, -most), most).astype(kind)


def setup_inputs(seed: int = 0) -> dict:
    streams_of = jax.random.split(jax.random.key(seed), 15)
    inputs = noise(streams_of[0], (SEQ_LEN, SEQUENCES, D), 1.0, 6.0, ((0, 4), (1, 2)))
    cotangent = noise(streams_of[1], (SEQ_LEN, SEQUENCES, D), 1.0, 6.0, ((0, 4), (1, 2)))
    ln1_gain = jnp.clip(1.0 + 0.1 * jax.random.normal(streams_of[2], (D,), jnp.float32), 0.5, 1.5).astype(jnp.bfloat16)
    ln1_bias = noise(streams_of[3], (D,), 0.3, 4.0, ((0, 2),))
    qkv_weight = noise(streams_of[4], (3, D, D), (D // 2) ** -0.5, 0.25, ((1, 2), (2, 4)))
    qv_bias = noise(streams_of[5], (2, HEADS, HD), 0.5, 6.0, ((1, 4), (2, 2)))
    proj_weight = noise(streams_of[6], (D, D), (max(4, D * 256 // SEQ_LEN)) ** -0.5, 0.375, ((0, 4), (1, 2)))
    proj_bias = noise(streams_of[7], (D,), 0.3, 4.0, ((0, 2),))
    ln2_gain = jnp.clip(1.0 + 0.1 * jax.random.normal(streams_of[8], (D,), jnp.float32), 0.5, 1.5).astype(jnp.bfloat16)
    ln2_bias = noise(streams_of[9], (D,), 0.3, 4.0, ((0, 2),))
    fc_weight = noise(streams_of[10], (D, FF), D ** -0.5, 0.1875, ((0, 2), (1, 4)))
    fc_bias = noise(streams_of[11], (FF // 64, 64), 0.5, 6.0, ((0, 4), (1, 2)))
    fc2_weight = noise(streams_of[12], (FF, D), FF ** -0.5, 0.09375, ((0, 4), (1, 2)))
    fc2_bias = noise(streams_of[13], (D,), 0.3, 4.0, ((0, 2),))
    return dict(inputs=inputs, cotangent=cotangent, ln1_gain=ln1_gain, ln1_bias=ln1_bias, qkv_weight=qkv_weight, qv_bias=qv_bias, proj_weight=proj_weight, proj_bias=proj_bias, ln2_gain=ln2_gain, ln2_bias=ln2_bias, fc_weight=fc_weight, fc_bias=fc_bias, fc2_weight=fc2_weight, fc2_bias=fc2_bias)


EPSILON = 1e-05
HIGHEST = lax.Precision.HIGHEST
NEGATIVE = -1e+30

@jax.custom_vjp
def low(v):
    return lax.optimization_barrier(v.astype(jnp.bfloat16)).astype(jnp.float32)

@jax.custom_vjp
def low_back(v):
    return v

def low_keep(v):
    return (low(v), None)

def low_pass(kept, grad):
    return (grad,)

def back_keep(v):
    return (v, None)

def back_low(kept, grad):
    return (low(grad),)
low.defvjp(low_keep, low_pass)
low_back.defvjp(back_keep, back_low)

def layer_norm(values, gain, shift):
    centred = values - lax.optimization_barrier(jnp.mean(values, axis=-1, keepdims=True))
    spread = lax.rsqrt(lax.optimization_barrier(jnp.mean(centred * centred, axis=-1, keepdims=True)) + EPSILON)
    return centred * spread * gain + shift

def matmul(left, right):
    return jnp.dot(left, right, precision=HIGHEST)

def one_sequence(params, sequence):
    gain_one, shift_one, qkv_full, bias_qv, proj_full, bias_proj, gain_two, shift_two, fc_full, bias_fc, fc2_full, bias_fc2 = params
    length = sequence.shape[0]
    first_in = low(layer_norm(sequence, gain_one, shift_one))
    bias_rows = bias_qv.reshape(2, D)
    query_rows = low(low_back(matmul(first_in, qkv_full[0]) + bias_rows[0]))
    key_rows = low(low_back(matmul(first_in, qkv_full[1])))
    value_rows = low(low_back(matmul(first_in, qkv_full[2]) + bias_rows[1]))
    key_heads = key_rows.reshape(length, HEADS, HD)
    value_heads = value_rows.reshape(length, HEADS, HD)
    key_blocks = jnp.arange(length, dtype=jnp.int32) // BLOCK

    @jax.checkpoint
    def attend(block_query, block_index):
        scores = low_back(jnp.einsum('qhd,khd->hqk', block_query, key_heads, precision=HIGHEST) * HD ** (-0.5))
        allowed = key_blocks[None, None, :] <= block_index
        scores = jnp.where(allowed, scores, NEGATIVE)
        row_peak = lax.optimization_barrier(jnp.max(scores, axis=-1, keepdims=True))
        exp_scores = jnp.where(allowed, jnp.exp(scores - row_peak), 0.0)
        attn_prob = exp_scores / lax.optimization_barrier(jnp.sum(exp_scores, axis=-1, keepdims=True))
        return jnp.einsum('hqk,khd->qhd', low(attn_prob), value_heads, precision=HIGHEST)
    block_count = length // BLOCK
    query_blocks = query_rows.reshape(block_count, BLOCK, HEADS, HD)
    block_ids = jnp.arange(block_count, dtype=jnp.int32)
    stacked = lax.map(lambda item: attend(item[0], item[1]), (query_blocks, block_ids))
    attended = low(low_back(stacked.reshape(length, D)))
    mixed = sequence + low_back(matmul(attended, proj_full) + bias_proj)
    second_in = low(layer_norm(mixed, gain_two, shift_two))
    pre_act = low_back(matmul(second_in, fc_full) + bias_fc.reshape(FF))
    hidden = low(jax.nn.gelu(pre_act, approximate=True))
    return mixed + low_back(matmul(hidden, fc2_full) + bias_fc2)

def forward(inputs, params):
    result = lax.map(functools.partial(one_sequence, params), jnp.moveaxis(inputs, 1, 0))
    return jnp.moveaxis(result, 0, 1)

def reference(inputs, cotangent, ln1_gain, ln1_bias, qkv_weight, qv_bias, proj_weight, proj_bias, ln2_gain, ln2_bias, fc_weight, fc_bias, fc2_weight, fc2_bias):
    params = tuple((entry.astype(jnp.float32) for entry in (ln1_gain, ln1_bias, qkv_weight, qv_bias, proj_weight, proj_bias, ln2_gain, ln2_bias, fc_weight, fc_bias, fc2_weight, fc2_bias)))
    output, pullback = jax.vjp(forward, inputs.astype(jnp.float32), params)
    input_grad, grads = pullback(cotangent.astype(jnp.float32))
    return (output.astype(jnp.bfloat16), input_grad.astype(jnp.bfloat16), grads[0], grads[1], grads[2], grads[3], grads[4], grads[5], grads[6], grads[7], grads[8], grads[9], grads[10], grads[11])
```

```python
from functools import partial
import math

import jax
import jax.numpy as jnp
from jax import lax
from jax.experimental import pallas as pl
from jax.experimental.pallas import tpu as pltpu
from jax.sharding import PartitionSpec as P


HD = 64
BLOCK = 256


EPSILON = 1e-05
NEGATIVE = -1e30
SUB_ROWS = 512


def norm_forward(values, gain, shift):
    centred = values - jnp.mean(values, axis=-1, keepdims=True)
    spread = lax.rsqrt(jnp.mean(centred * centred, axis=-1, keepdims=True) + EPSILON)
    normed = centred * spread
    return (normed * gain + shift, normed, spread)


def norm_backward(grad_out, normed, spread, gain):
    scaled = grad_out * gain
    return spread * (
        scaled
        - jnp.mean(scaled, axis=-1, keepdims=True)
        - normed * jnp.mean(scaled * normed, axis=-1, keepdims=True)
    )


def left_inner(left, right):
    return lax.dot_general(
        left, right, (((0,), (0,)), ((), ())), preferred_element_type=jnp.float32
    )


def right_inner(left, right):
    return lax.dot_general(
        left, right, (((1,), (1,)), ((), ())), preferred_element_type=jnp.float32
    )


def split_heads(values):
    return values.reshape(values.shape[0], values.shape[1], -1, HD)


def block_scores(query_heads, key_heads, query_pos, key_pos):
    scores = jnp.einsum(
        "qshd,kshd->qshk", query_heads, key_heads, preferred_element_type=jnp.float32
    ) * HD ** (-0.5)
    allowed = key_pos[None, :] // BLOCK <= query_pos[:, None] // BLOCK
    return (scores, allowed[:, None, None, :])


def by_blocks(step_fn, carry, pieces):
    count = pieces[0].shape[0]
    sub_width = math.gcd(count, SUB_ROWS)
    split = tuple(
        (entry.reshape((count // sub_width, sub_width) + entry.shape[1:]) for entry in pieces)
    )

    def advance(state, item):
        block_index, parts = item
        return (step_fn(state, parts, block_index * sub_width), None)

    state, unused = lax.scan(
        advance, carry, (jnp.arange(count // sub_width, dtype=jnp.int32), split)
    )
    return state


def general_device(
    inputs,
    cotangent,
    ln1_gain,
    ln1_bias,
    qkv_weight,
    qv_bias,
    proj_weight,
    proj_bias,
    ln2_gain,
    ln2_bias,
    fc_weight,
    fc_bias,
    fc2_weight,
    fc2_bias,
):
    row_count, seq_count, model_width = inputs.shape
    tokens = row_count * seq_count
    tp_count = lax.axis_size("tp")
    share_rows = row_count // tp_count
    share_tokens = share_rows * seq_count
    share_first = lax.axis_index("tp") * share_tokens

    def own_rows(values):
        return lax.dynamic_slice_in_dim(values, share_first, share_tokens, 0)

    gathered = (
        lax.all_gather(ln1_gain, "fsdp", axis=0, tiled=True),
        lax.all_gather(ln1_bias, "fsdp", axis=0, tiled=True),
        lax.all_gather(qkv_weight, "fsdp", axis=1, tiled=True),
        lax.all_gather(qv_bias, "fsdp", axis=2, tiled=True),
        lax.all_gather(proj_weight, "fsdp", axis=1, tiled=True),
        lax.all_gather(proj_bias, "fsdp", axis=0, tiled=True),
        lax.all_gather(ln2_gain, "fsdp", axis=0, tiled=True),
        lax.all_gather(ln2_bias, "fsdp", axis=0, tiled=True),
        lax.all_gather(fc_weight, "fsdp", axis=0, tiled=True),
        lax.all_gather(fc_bias, "fsdp", axis=1, tiled=True),
        lax.all_gather(fc2_weight, "fsdp", axis=1, tiled=True),
        lax.all_gather(fc2_bias, "fsdp", axis=0, tiled=True),
    )
    (
        gain_one,
        shift_one,
        qkv_full,
        bias_qv,
        proj_full,
        bias_proj,
        gain_two,
        shift_two,
        fc_full,
        bias_fc,
        fc2_full,
        bias_fc2,
    ) = gathered
    head_width = qkv_full.shape[2]
    gain_one_f = gain_one.astype(jnp.float32)
    gain_two_f = gain_two.astype(jnp.float32)
    flat = inputs.reshape(tokens, model_width).astype(jnp.float32)
    first_f, normed_one, spread_one = norm_forward(flat, gain_one_f, shift_one.astype(jnp.float32))
    first_in = first_f.astype(jnp.bfloat16)
    bias_rows = bias_qv.reshape(2, head_width).astype(jnp.float32)
    projected = jnp.einsum("td,cdf->ctf", first_in, qkv_full, preferred_element_type=jnp.float32)
    query_three = (
        (projected[0] + bias_rows[0]).astype(jnp.bfloat16).reshape(row_count, seq_count, head_width)
    )
    key_three = projected[1].astype(jnp.bfloat16).reshape(row_count, seq_count, head_width)
    value_three = (
        (projected[2] + bias_rows[1]).astype(jnp.bfloat16).reshape(row_count, seq_count, head_width)
    )
    query_heads = split_heads(query_three)
    key_heads = split_heads(key_three)
    value_heads = split_heads(value_three)
    local_heads = query_heads.shape[2]
    cycle_place = lax.axis_index("ctx")
    my_first = cycle_place * row_count
    my_pos = my_first + jnp.arange(row_count, dtype=jnp.int32)
    last_block = (my_first + row_count - 1) // BLOCK
    scale = HD ** (-0.5)

    def forward_step(state, parts, first_row):
        key_part, value_part = parts
        key_pos = first_row + jnp.arange(key_part.shape[0], dtype=jnp.int32)

        def update(inner):
            acc_sum, row_top, denom_sum = inner
            scores, allowed = block_scores(query_heads, split_heads(key_part), my_pos, key_pos)
            scores = jnp.where(allowed, scores, NEGATIVE)
            new_top = jnp.maximum(row_top, jnp.max(scores, axis=-1))
            rescale = jnp.exp(row_top - new_top)
            block_weights = jnp.where(allowed, jnp.exp(scores - new_top[..., None]), 0.0)
            denom_sum = denom_sum * rescale + jnp.sum(block_weights, axis=-1)
            acc_sum = acc_sum * rescale[..., None] + jnp.einsum(
                "qshk,kshd->qshd",
                block_weights.astype(jnp.bfloat16),
                split_heads(value_part),
                preferred_element_type=jnp.float32,
            )
            return (acc_sum, new_top, denom_sum)

        return lax.cond(first_row // BLOCK > last_block, lambda inner: inner, update, state)

    stat_shape = (row_count, seq_count, local_heads)
    start_state = (
        jnp.zeros(query_heads.shape, jnp.float32),
        jnp.full(stat_shape, NEGATIVE, jnp.float32),
        jnp.zeros(stat_shape, jnp.float32),
    )
    acc_sum, row_top, denom_sum = by_blocks(
        forward_step,
        start_state,
        (
            lax.all_gather(key_three, "ctx", axis=0, tiled=True),
            lax.all_gather(value_three, "ctx", axis=0, tiled=True),
        ),
    )
    attended_f = acc_sum / denom_sum[..., None]
    log_total = row_top + jnp.log(denom_sum)
    attended = attended_f.reshape(tokens, head_width).astype(jnp.bfloat16)
    attn_term = jnp.dot(attended, proj_full, preferred_element_type=jnp.float32)
    mixed_rows = flat + lax.psum(attn_term, "tp") + bias_proj.astype(jnp.float32)
    second_f, normed_two, spread_two = norm_forward(
        mixed_rows, gain_two_f, shift_two.astype(jnp.float32)
    )
    second_in = second_f.astype(jnp.bfloat16)
    pre_act = jnp.dot(second_in, fc_full, preferred_element_type=jnp.float32) + bias_fc.reshape(
        -1
    ).astype(jnp.float32)
    activated, gelu_pull = jax.vjp(partial(jax.nn.gelu, approximate=True), pre_act)
    hidden = activated.astype(jnp.bfloat16)
    mlp_term = jnp.dot(hidden, fc2_full, preferred_element_type=jnp.float32)
    final_share = own_rows(mixed_rows + lax.psum(mlp_term, "tp") + bias_fc2.astype(jnp.float32))
    output = final_share.astype(jnp.bfloat16).reshape(share_rows, seq_count, model_width)
    grad_rows = cotangent.reshape(tokens, model_width)
    grad_y = grad_rows.astype(jnp.float32)
    grad_bias_fc2 = jnp.sum(grad_y, axis=0)
    grad_fc2 = left_inner(hidden, grad_rows)
    hidden_grad = right_inner(grad_rows, fc2_full)
    (pre_grad_f,) = gelu_pull(hidden_grad)
    pre_grad = pre_grad_f.astype(jnp.bfloat16)
    grad_bias_fc = jnp.sum(pre_grad.astype(jnp.float32), axis=0)
    grad_fc = left_inner(second_in, pre_grad)
    second_term = right_inner(pre_grad, fc_full)
    second_grad = lax.psum(second_term, "tp")
    grad_gain_two = jnp.sum(second_grad * normed_two, axis=0)
    grad_shift_two = jnp.sum(second_grad, axis=0)
    mixed_grad = grad_y + norm_backward(second_grad, normed_two, spread_two, gain_two_f)
    branch_grad = mixed_grad.astype(jnp.bfloat16)
    grad_bias_proj = jnp.sum(branch_grad.astype(jnp.float32), axis=0)
    grad_proj = left_inner(attended, branch_grad)
    attended_grad = right_inner(branch_grad, proj_full).astype(jnp.bfloat16)
    grad_three = attended_grad.reshape(row_count, seq_count, head_width)
    grad_heads = split_heads(grad_three)
    delta_rows = jnp.sum(grad_heads.astype(jnp.float32) * attended_f, axis=-1)
    lse_all, delta_all = (
        lax.all_gather(log_total, "ctx", axis=0, tiled=True),
        lax.all_gather(delta_rows, "ctx", axis=0, tiled=True),
    )

    def back_step(state, parts, first_row):
        query_part_flat, key_part_flat, value_part_flat, grad_part_flat = parts
        count = query_part_flat.shape[0]
        other_pos = first_row + jnp.arange(count, dtype=jnp.int32)
        query_acc, key_acc, value_acc = state

        def query_update(acc_in):
            key_part = split_heads(key_part_flat)
            scores, allowed = block_scores(query_heads, key_part, my_pos, other_pos)
            attn_prob = jnp.where(allowed, jnp.exp(scores - log_total[..., None]), 0.0)
            prob_grad = jnp.einsum(
                "qshd,kshd->qshk",
                grad_heads,
                split_heads(value_part_flat),
                preferred_element_type=jnp.float32,
            )
            score_grad = (attn_prob * (prob_grad - delta_rows[..., None])).astype(jnp.bfloat16)
            return (
                acc_in
                + jnp.einsum(
                    "qshk,kshd->qshd", score_grad, key_part, preferred_element_type=jnp.float32
                )
                * scale
            )

        def key_update(inner):
            key_in, value_in = inner
            lse_part = lax.dynamic_slice_in_dim(lse_all, first_row, count, 0)
            delta_part = lax.dynamic_slice_in_dim(delta_all, first_row, count, 0)
            query_part = split_heads(query_part_flat)
            grad_part = split_heads(grad_part_flat)
            scores, allowed = block_scores(query_part, key_heads, other_pos, my_pos)
            attn_prob = jnp.where(allowed, jnp.exp(scores - lse_part[..., None]), 0.0)
            prob_grad = jnp.einsum(
                "qshd,kshd->qshk", grad_part, value_heads, preferred_element_type=jnp.float32
            )
            score_grad = (attn_prob * (prob_grad - delta_part[..., None])).astype(jnp.bfloat16)
            key_in = (
                key_in
                + jnp.einsum(
                    "qshk,qshd->kshd", score_grad, query_part, preferred_element_type=jnp.float32
                )
                * scale
            )
            value_in = value_in + jnp.einsum(
                "qshk,qshd->kshd",
                attn_prob.astype(jnp.bfloat16),
                grad_part,
                preferred_element_type=jnp.float32,
            )
            return (key_in, value_in)

        query_acc = lax.cond(
            first_row // BLOCK > last_block, lambda acc_in: acc_in, query_update, query_acc
        )
        key_acc, value_acc = lax.cond(
            my_first // BLOCK > (first_row + count - 1) // BLOCK,
            lambda inner: inner,
            key_update,
            (key_acc, value_acc),
        )
        return (query_acc, key_acc, value_acc)

    zero_heads = jnp.zeros(query_heads.shape, jnp.float32)
    query_grad_f, key_grad_f, value_grad_f = by_blocks(
        back_step,
        (zero_heads, zero_heads, zero_heads),
        (
            lax.all_gather(query_three, "ctx", axis=0, tiled=True),
            lax.all_gather(key_three, "ctx", axis=0, tiled=True),
            lax.all_gather(value_three, "ctx", axis=0, tiled=True),
            lax.all_gather(grad_three, "ctx", axis=0, tiled=True),
        ),
    )
    query_grad = query_grad_f.reshape(tokens, head_width).astype(jnp.bfloat16)
    key_grad = key_grad_f.reshape(tokens, head_width).astype(jnp.bfloat16)
    value_grad = value_grad_f.reshape(tokens, head_width).astype(jnp.bfloat16)
    stacked_grad = jnp.stack([query_grad, key_grad, value_grad])
    grad_bias_qv = jnp.stack(
        [
            jnp.sum(query_grad.astype(jnp.float32), axis=0),
            jnp.sum(value_grad.astype(jnp.float32), axis=0),
        ]
    ).reshape(bias_qv.shape)
    grad_qkv = jnp.einsum("td,ctf->cdf", first_in, stacked_grad, preferred_element_type=jnp.float32)
    first_term = jnp.einsum(
        "ctf,cdf->td", stacked_grad, qkv_full, preferred_element_type=jnp.float32
    )
    first_grad = lax.psum(first_term, "tp")
    grad_gain_one = jnp.sum(first_grad * normed_one, axis=0)
    grad_shift_one = jnp.sum(first_grad, axis=0)
    input_rows = own_rows(
        mixed_grad + norm_backward(first_grad, normed_one, spread_one, gain_one_f)
    )
    input_grad = input_rows.astype(jnp.bfloat16).reshape(share_rows, seq_count, model_width)
    shares = (
        lax.psum_scatter(grad_gain_one, ("fsdp", "ctx"), scatter_dimension=0, tiled=True),
        lax.psum_scatter(grad_shift_one, ("fsdp", "ctx"), scatter_dimension=0, tiled=True),
        lax.psum_scatter(grad_qkv, ("fsdp", "ctx"), scatter_dimension=1, tiled=True),
        lax.psum_scatter(grad_bias_qv, ("fsdp", "ctx"), scatter_dimension=2, tiled=True),
        lax.psum_scatter(grad_proj, ("fsdp", "ctx"), scatter_dimension=1, tiled=True),
        lax.psum_scatter(grad_bias_proj, ("fsdp", "ctx"), scatter_dimension=0, tiled=True),
        lax.psum_scatter(grad_gain_two, ("fsdp", "ctx"), scatter_dimension=0, tiled=True),
        lax.psum_scatter(grad_shift_two, ("fsdp", "ctx"), scatter_dimension=0, tiled=True),
        lax.psum_scatter(grad_fc, ("fsdp", "ctx"), scatter_dimension=0, tiled=True),
        lax.psum_scatter(
            grad_bias_fc.reshape(bias_fc.shape), ("fsdp", "ctx"), scatter_dimension=1, tiled=True
        ),
        lax.psum_scatter(grad_fc2, ("fsdp", "ctx"), scatter_dimension=1, tiled=True),
        lax.psum_scatter(grad_bias_fc2, ("fsdp", "ctx"), scatter_dimension=0, tiled=True),
    )
    summed = (
        lax.all_gather(shares[0], "ctx", axis=0, tiled=True),
        lax.all_gather(shares[1], "ctx", axis=0, tiled=True),
        lax.all_gather(shares[2], "ctx", axis=1, tiled=True),
        lax.all_gather(shares[3], "ctx", axis=2, tiled=True),
        lax.all_gather(shares[4], "ctx", axis=1, tiled=True),
        lax.all_gather(shares[5], "ctx", axis=0, tiled=True),
        lax.all_gather(shares[6], "ctx", axis=0, tiled=True),
        lax.all_gather(shares[7], "ctx", axis=0, tiled=True),
        lax.all_gather(shares[8], "ctx", axis=0, tiled=True),
        lax.all_gather(shares[9], "ctx", axis=1, tiled=True),
        lax.all_gather(shares[10], "ctx", axis=1, tiled=True),
        lax.all_gather(shares[11], "ctx", axis=0, tiled=True),
    )
    return (
        output,
        input_grad,
        summed[0],
        summed[1],
        summed[2],
        summed[3],
        summed[4],
        summed[5],
        summed[6],
        summed[7],
        summed[8],
        summed[9],
        summed[10],
        summed[11],
    )


SWAP = ((0, 1), (1, 0))
MATE = ((0, 1), (1, 0), (2, 3), (3, 2))
PEER = ((0, 2), (2, 0), (1, 3), (3, 1))
INWARD = ((0, 1), (3, 2))
MIDDLE = ((1, 2), (2, 1))
OUTWARD = ((1, 0), (2, 3))


def xor_pairs(count, mask):
    return tuple((place, place ^ mask) for place in range(count))


def bf(values):
    return values.astype(jnp.bfloat16)


def f32(values):
    return values.astype(jnp.float32)


def matmul(left, right):
    return jnp.dot(left, right, preferred_element_type=jnp.float32)


def contract(left, right, left_dim, right_dim):
    return lax.dot_general(
        left,
        right,
        (((left_dim,), (right_dim,)), ((), ())),
        preferred_element_type=jnp.float32,
    )


def merged(values):
    return values.reshape(-1, values.shape[-1])


def attend_kernel(query_ref, key_ref, value_ref, out_ref, lse_ref, score_ref, acc_ref):
    block = pl.program_id(0)
    query = merged(query_ref[:, 0])
    rows, width = query.shape
    lane_head = lax.broadcasted_iota(jnp.int32, (rows, width), 1) // HD
    scale = HD ** (-0.5)
    acc_ref[...] = jnp.zeros_like(acc_ref)

    def one_head(head, unused):
        mine = lane_head == head
        query_h = jnp.where(mine, query, jnp.zeros_like(query))

        def score(other, top):
            values = contract(merged(key_ref[:, other]), query_h, 1, 1)
            score_ref[other] = values
            return jnp.maximum(top, jnp.max(values, axis=0, keepdims=True))

        top = lax.fori_loop(0, block + 1, score, jnp.full((1, rows), NEGATIVE, jnp.float32))

        def weigh(other, total):
            values = jnp.exp((score_ref[other] - top) * scale)
            score_ref[other] = values
            return total + jnp.sum(values, axis=0, keepdims=True)

        total = lax.fori_loop(0, block + 1, weigh, jnp.zeros((1, rows), jnp.float32))
        lse_ref[0, head] = top * scale + jnp.log(total)
        inverse = 1.0 / total

        def mix(other, unused_two):
            value = merged(value_ref[:, other])
            value_h = jnp.where(mine, value, jnp.zeros_like(value))
            acc_ref[...] += contract(bf(score_ref[other] * inverse), value_h, 0, 0)
            return unused_two

        lax.fori_loop(0, block + 1, mix, 0)
        return unused

    lax.fori_loop(0, width // HD, one_head, 0)
    out_ref[:, 0] = bf(acc_ref[...]).reshape(out_ref.shape[0], out_ref.shape[2], width)


def attend_back_kernel(
    query_ref,
    key_ref,
    value_ref,
    out_ref,
    grad_ref,
    lse_ref,
    query_grad_ref,
    key_grad_ref,
    value_grad_ref,
    query_acc,
    key_acc,
    value_acc,
):
    block = pl.program_id(0)
    blocks = pl.num_programs(0)
    query = merged(query_ref[:, 0])
    grad = merged(grad_ref[:, 0])
    rows, width = query.shape
    lane_head = lax.broadcasted_iota(jnp.int32, (rows, width), 1) // HD
    scale = HD ** (-0.5)
    products = f32(grad) * f32(merged(out_ref[:, 0]))
    query_acc[...] = jnp.zeros_like(query_acc)

    @pl.when(block == 0)
    def clear():
        key_acc[...] = jnp.zeros_like(key_acc)
        value_acc[...] = jnp.zeros_like(value_acc)

    def one_head(head, unused):
        mine = lane_head == head
        query_h = jnp.where(mine, query, jnp.zeros_like(query))
        grad_h = jnp.where(mine, grad, jnp.zeros_like(grad))
        delta_column = jnp.sum(jnp.where(mine, products, 0.0), axis=1, keepdims=True)
        delta = jnp.transpose(jnp.broadcast_to(delta_column, (rows, 128)))[0:1]
        lse = lse_ref[0, head]

        def one_block(other, unused_two):
            key = merged(key_ref[:, other])
            key_h = jnp.where(mine, key, jnp.zeros_like(key))
            scores = contract(key, query_h, 1, 1)
            prob_grad = contract(merged(value_ref[:, other]), grad_h, 1, 1)
            prob = jnp.exp(scores * scale - lse)
            score_grad = bf(prob * (prob_grad - delta))
            value_acc[other] += contract(bf(prob), grad_h, 1, 0)
            key_acc[other] += contract(score_grad, query_h, 1, 0)
            query_acc[...] += contract(score_grad, key_h, 0, 0)
            return unused_two

        lax.fori_loop(0, block + 1, one_block, 0)
        return unused

    lax.fori_loop(0, width // HD, one_head, 0)
    shape = (query_grad_ref.shape[0], query_grad_ref.shape[2], width)
    query_grad_ref[:, 0] = bf(query_acc[...] * scale).reshape(shape)

    @pl.when(block == blocks - 1)
    def finish():
        for other in range(key_acc.shape[0]):
            key_grad_ref[:, other] = bf(key_acc[other] * scale).reshape(shape)
            value_grad_ref[:, other] = bf(value_acc[other]).reshape(shape)


def attend(query, key, value):
    slots, blocks, part, width = query.shape
    rows = slots * part
    heads = width // HD
    one = pl.BlockSpec((slots, 1, part, width), lambda i: (0, i, 0, 0))
    whole = pl.BlockSpec((slots, blocks, part, width), lambda i: (0, 0, 0, 0))
    pairs = blocks * (blocks + 1) // 2 * heads
    return pl.pallas_call(
        attend_kernel,
        grid=(blocks,),
        in_specs=[one, whole, whole],
        out_specs=[one, pl.BlockSpec((1, heads, 1, rows), lambda i: (i, 0, 0, 0))],
        out_shape=[
            jax.ShapeDtypeStruct(query.shape, jnp.bfloat16),
            jax.ShapeDtypeStruct((blocks, heads, 1, rows), jnp.float32),
        ],
        scratch_shapes=[
            pltpu.VMEM((blocks, rows, rows), jnp.float32),
            pltpu.VMEM((rows, width), jnp.float32),
        ],
        cost_estimate=pl.CostEstimate(
            flops=pairs * 4 * rows * rows * width,
            bytes_accessed=4 * query.size * 2,
            transcendentals=pairs * rows * rows,
        ),
        name="attend",
    )(query, key, value)


def attend_back(query, key, value, out, grad, lse):
    slots, blocks, part, width = query.shape
    rows = slots * part
    heads = width // HD
    one = pl.BlockSpec((slots, 1, part, width), lambda i: (0, i, 0, 0))
    whole = pl.BlockSpec((slots, blocks, part, width), lambda i: (0, 0, 0, 0))
    pairs = blocks * (blocks + 1) // 2 * heads
    return pl.pallas_call(
        attend_back_kernel,
        grid=(blocks,),
        in_specs=[
            one,
            whole,
            whole,
            one,
            one,
            pl.BlockSpec((1, heads, 1, rows), lambda i: (i, 0, 0, 0)),
        ],
        out_specs=[one, whole, whole],
        out_shape=[jax.ShapeDtypeStruct(query.shape, jnp.bfloat16)] * 3,
        scratch_shapes=[
            pltpu.VMEM((rows, width), jnp.float32),
            pltpu.VMEM((blocks, rows, width), jnp.float32),
            pltpu.VMEM((blocks, rows, width), jnp.float32),
        ],
        cost_estimate=pl.CostEstimate(
            flops=pairs * 10 * rows * rows * width,
            bytes_accessed=8 * query.size * 2,
            transcendentals=pairs * rows * rows,
        ),
        name="attend_back",
    )(query, key, value, out, grad, lse)


def spread_parts(values):
    mate = lax.ppermute(values, "tp", MATE)
    peer = lax.ppermute(values, "tp", PEER)
    across = lax.ppermute(peer, "tp", MATE)
    return (values, mate, peer, across)


def spread_rows(values):
    return jnp.concatenate(spread_parts(values), axis=0)


def gather_sum(part_of):
    across = lax.ppermute(bf(part_of(3)), "tp", MATE)
    peer = lax.ppermute(bf(part_of(2) + f32(across)), "tp", PEER)
    mate = lax.ppermute(bf(part_of(1)), "tp", MATE)
    return part_of(0) + f32(mate) + f32(peer)


def sum_weight(kept, sent):
    half = kept + f32(lax.ppermute(bf(sent), "fsdp", SWAP))
    pair = bf(half + f32(lax.ppermute(bf(half), "ctx", INWARD)))
    total = bf(f32(pair) + f32(lax.ppermute(pair, "ctx", MIDDLE)))
    outer = lax.ppermute(total, "ctx", OUTWARD)
    place = lax.axis_index("ctx")
    inner = jnp.logical_and(place > 0, place < 3)
    return f32(jnp.where(inner, total, outer))


def fast_device(
    inputs,
    cotangent,
    ln1_gain,
    ln1_bias,
    qkv_weight,
    qv_bias,
    proj_weight,
    proj_bias,
    ln2_gain,
    ln2_bias,
    fc_weight,
    fc_bias,
    fc2_weight,
    fc2_bias,
):
    row_count, seq_count, width = inputs.shape
    tp_count = lax.axis_size("tp")
    ctx_count = lax.axis_size("ctx")
    share_rows = row_count // tp_count
    share_tokens = share_rows * ctx_count
    place_f = lax.axis_index("fsdp")
    place_c = lax.axis_index("ctx")
    place_t = lax.axis_index("tp")
    half = width // 2
    lower = place_f == 0

    def own_first(values):
        flipped = jnp.concatenate([values[..., half:], values[..., :half]], axis=-1)
        return jnp.where(lower, values, flipped)

    def join(own, other, axis):
        return jnp.where(
            lower,
            jnp.concatenate([own, other], axis=axis),
            jnp.concatenate([other, own], axis=axis),
        )

    def to_sequences(values):
        mine = lax.dynamic_slice_in_dim(values, place_t * share_rows, share_rows, 0)
        mine = own_first(mine)
        got = []
        for step in range(ctx_count):
            piece = lax.dynamic_index_in_dim(mine, place_c ^ step, 1, keepdims=False)
            if step:
                piece = lax.ppermute(piece, "ctx", xor_pairs(ctx_count, step))
            got.append(piece)
        stacked = jnp.stack(got)
        ordered = [
            lax.dynamic_index_in_dim(stacked, place_c ^ step, 0, keepdims=False)
            for step in range(ctx_count)
        ]
        return jnp.concatenate(ordered, axis=0)

    def to_positions(values):
        mine = own_first(values).reshape(ctx_count, share_rows, width)
        got = []
        for step in range(ctx_count):
            piece = lax.dynamic_index_in_dim(mine, place_c ^ step, 0, keepdims=False)
            if step:
                piece = lax.ppermute(piece, "ctx", xor_pairs(ctx_count, step))
            got.append(piece)
        stacked = jnp.stack(got)
        ordered = [
            lax.dynamic_index_in_dim(stacked, place_c ^ step, 0, keepdims=False)
            for step in range(ctx_count)
        ]
        return jnp.stack(ordered, axis=1)

    flat = f32(to_sequences(inputs))

    small_own = jnp.concatenate(
        [
            jnp.stack([ln1_gain, ln1_bias, proj_bias, ln2_gain, ln2_bias, fc2_bias]).reshape(-1),
            qv_bias.reshape(-1),
            fc_bias.reshape(-1),
        ]
    ).reshape(-1, 128)
    small_other = lax.ppermute(small_own, "fsdp", SWAP)
    qkv_other = lax.ppermute(qkv_weight, "fsdp", SWAP)
    proj_other = lax.ppermute(proj_weight, "fsdp", SWAP)
    fc_other = lax.ppermute(fc_weight, "fsdp", SWAP)
    fc2_other = lax.ppermute(fc2_weight, "fsdp", SWAP)
    qkv_full = jnp.concatenate([qkv_weight, qkv_other], axis=1)
    proj_full = jnp.concatenate([proj_weight, proj_other], axis=1)
    fc_full = jnp.concatenate([fc_weight, fc_other], axis=0)
    fc2_full = jnp.concatenate([fc2_weight, fc2_other], axis=1)

    small_own = small_own.reshape(-1)
    small_other = small_other.reshape(-1)
    vectors = f32(
        jnp.concatenate(
            [small_own[: 6 * half].reshape(6, half), small_other[: 6 * half].reshape(6, half)],
            axis=1,
        )
    )
    gain_one, shift_one, bias_proj, gain_two, shift_two, bias_fc2 = (vectors[n] for n in range(6))
    qv_end = 6 * half + qv_bias.size
    bias_qv = f32(
        join(
            small_own[6 * half : qv_end].reshape(qv_bias.shape),
            small_other[6 * half : qv_end].reshape(qv_bias.shape),
            2,
        )
    )
    bias_fc = f32(
        join(
            small_own[qv_end:].reshape(fc_bias.shape),
            small_other[qv_end:].reshape(fc_bias.shape),
            1,
        )
    )
    head_width = qkv_full.shape[2]
    bias_rows = bias_qv.reshape(2, head_width)

    first_f, normed_one, spread_one = norm_forward(flat, gain_one, shift_one)
    first_in = spread_rows(bf(first_f))
    projected = jnp.einsum("td,cdf->ctf", first_in, qkv_full, preferred_element_type=jnp.float32)
    head_shape = (tp_count, ctx_count, share_rows, head_width)
    query = bf(projected[0] + bias_rows[0]).reshape(head_shape)
    key = bf(projected[1]).reshape(head_shape)
    value = bf(projected[2] + bias_rows[1]).reshape(head_shape)
    attended_four, lse = attend(query, key, value)
    attended = attended_four.reshape(-1, head_width)

    def rows_of(values, slot):
        return values[slot * share_tokens : (slot + 1) * share_tokens]

    attn_sum = gather_sum(lambda slot: matmul(rows_of(attended, slot), proj_full))
    mixed = flat + attn_sum + bias_proj
    second_f, normed_two, spread_two = norm_forward(mixed, gain_two, shift_two)
    second_in = spread_rows(bf(second_f))

    grad_own = to_sequences(cotangent)
    grad_rows = spread_rows(grad_own)
    grad_y = f32(grad_own)

    hidden_grad = contract(grad_rows, fc2_full, 1, 1)
    pre_act = matmul(second_in, fc_full) + bias_fc.reshape(-1)
    activated, gelu_pull = jax.vjp(partial(jax.nn.gelu, approximate=True), pre_act)
    hidden = bf(activated)
    (pre_grad_f,) = gelu_pull(hidden_grad)
    pre_grad = bf(pre_grad_f)

    second_grad = gather_sum(lambda slot: contract(rows_of(pre_grad, slot), fc_full, 1, 1))
    mixed_grad = grad_y + norm_backward(second_grad, normed_two, spread_two, gain_two)
    branch_own = bf(mixed_grad)
    branch = spread_rows(branch_own)

    mlp_sum = gather_sum(lambda slot: matmul(rows_of(hidden, slot), fc2_full))
    output = to_positions(bf(mixed + mlp_sum + bias_fc2))

    grad_fc2 = sum_weight(
        contract(hidden, grad_rows[:, :half], 0, 0), contract(hidden, grad_rows[:, half:], 0, 0)
    )
    grad_fc = sum_weight(
        contract(second_in[:, :half], pre_grad, 0, 0),
        contract(second_in[:, half:], pre_grad, 0, 0),
    )

    attended_grad = bf(contract(branch, proj_full, 1, 1)).reshape(head_shape)
    query_grad, key_grad, value_grad = (
        entry.reshape(-1, head_width)
        for entry in attend_back(query, key, value, attended_four, attended_grad, lse)
    )
    grad_proj = sum_weight(
        contract(attended, branch[:, :half], 0, 0), contract(attended, branch[:, half:], 0, 0)
    )

    def first_part(slot):
        return (
            contract(rows_of(query_grad, slot), qkv_full[0], 1, 1)
            + contract(rows_of(key_grad, slot), qkv_full[1], 1, 1)
            + contract(rows_of(value_grad, slot), qkv_full[2], 1, 1)
        )

    first_grad = gather_sum(first_part)
    input_own = mixed_grad + norm_backward(first_grad, normed_one, spread_one, gain_one)
    input_grad = to_positions(bf(input_own))

    def qkv_grads(columns):
        return jnp.stack(
            [contract(columns, entry, 0, 0) for entry in (query_grad, key_grad, value_grad)]
        )

    grad_qkv = sum_weight(qkv_grads(first_in[:, :half]), qkv_grads(first_in[:, half:]))

    token_sums = jnp.stack(
        [
            jnp.sum(first_grad * normed_one, axis=0),
            jnp.sum(first_grad, axis=0),
            jnp.sum(f32(branch_own), axis=0),
            jnp.sum(second_grad * normed_two, axis=0),
            jnp.sum(second_grad, axis=0),
            jnp.sum(grad_y, axis=0),
        ]
    )
    sum_qv = jnp.stack(
        [jnp.sum(f32(query_grad), axis=0), jnp.sum(f32(value_grad), axis=0)]
    ).reshape(bias_qv.shape)
    sum_fc = jnp.sum(f32(pre_grad), axis=0).reshape(bias_fc.shape)
    qv_part = qv_bias.shape[2]
    fc_part = fc_bias.shape[1]

    def small_pack(vector_half, which):
        return jnp.concatenate(
            [
                vector_half.reshape(-1),
                lax.dynamic_slice_in_dim(sum_qv, which * qv_part, qv_part, 2).reshape(-1),
                lax.dynamic_slice_in_dim(sum_fc, which * fc_part, fc_part, 1).reshape(-1),
            ]
        ).reshape(-1, 128)

    small = small_pack(token_sums[:, :half], place_f) + lax.ppermute(
        small_pack(token_sums[:, half:], 1 - place_f), "fsdp", SWAP
    )
    split = 6 * half // 128
    small_d = small[:split]
    small_d = small_d + lax.ppermute(small_d, "tp", MATE)
    small_d = small_d + lax.ppermute(small_d, "tp", PEER)
    small = jnp.concatenate([small_d, small[split:]], axis=0)
    small = small + lax.ppermute(small, "ctx", xor_pairs(ctx_count, 1))
    small = small + lax.ppermute(small, "ctx", xor_pairs(ctx_count, 2))
    small = small.reshape(-1)
    sums = small[: 6 * half].reshape(6, half)
    return (
        output,
        input_grad,
        sums[0],
        sums[1],
        grad_qkv,
        small[6 * half : qv_end].reshape(qv_bias.shape),
        grad_proj,
        sums[2],
        sums[3],
        sums[4],
        grad_fc,
        small[qv_end:].reshape(fc_bias.shape),
        grad_fc2,
        sums[5],
    )


def on_device(*args):
    rows, sequences, unused_width = args[0].shape
    whole_sequences = (
        lax.axis_size("fsdp") == 2
        and lax.axis_size("tp") == 4
        and lax.axis_size("ctx") == 4
        and sequences == 4
        and rows == BLOCK
    )
    return (fast_device if whole_sequences else general_device)(*args)


def solution(mesh):
    return jax.shard_map(
        on_device,
        mesh=mesh,
        in_specs=(
            P("ctx", "fsdp", None),
            P("ctx", "fsdp", None),
            P("fsdp"),
            P("fsdp"),
            P(None, "fsdp", "tp"),
            P(None, "tp", "fsdp"),
            P("tp", "fsdp"),
            P("fsdp"),
            P("fsdp"),
            P("fsdp"),
            P("fsdp", "tp"),
            P("tp", "fsdp"),
            P("tp", "fsdp"),
            P("fsdp"),
        ),
        out_specs=(
            P(("ctx", "tp"), "fsdp", None),
            P(("ctx", "tp"), "fsdp", None),
            P("fsdp"),
            P("fsdp"),
            P(None, "fsdp", "tp"),
            P(None, "tp", "fsdp"),
            P("tp", "fsdp"),
            P("fsdp"),
            P("fsdp"),
            P("fsdp"),
            P("fsdp", "tp"),
            P("tp", "fsdp"),
            P("tp", "fsdp"),
            P("fsdp"),
        ),
        check_vma=False,
    )
```

```python
from functools import partial
import math

import jax
import jax.numpy as jnp
from jax import lax
from jax.experimental import pallas as pl
from jax.experimental.pallas import tpu as pltpu
from jax.sharding import PartitionSpec as P


HD = 64
BLOCK = 256


EPSILON = 1e-05
NEGATIVE = -1e30
SUB_ROWS = 512


def norm_forward(values, gain, shift):
    centred = values - jnp.mean(values, axis=-1, keepdims=True)
    spread = lax.rsqrt(jnp.mean(centred * centred, axis=-1, keepdims=True) + EPSILON)
    normed = centred * spread
    return (normed * gain + shift, normed, spread)


def norm_backward(grad_out, normed, spread, gain):
    scaled = grad_out * gain
    return spread * (
        scaled
        - jnp.mean(scaled, axis=-1, keepdims=True)
        - normed * jnp.mean(scaled * normed, axis=-1, keepdims=True)
    )


def left_inner(left, right):
    return lax.dot_general(
        left, right, (((0,), (0,)), ((), ())), preferred_element_type=jnp.float32
    )


def right_inner(left, right):
    return lax.dot_general(
        left, right, (((1,), (1,)), ((), ())), preferred_element_type=jnp.float32
    )


def split_heads(values):
    return values.reshape(values.shape[0], values.shape[1], -1, HD)


def block_scores(query_heads, key_heads, query_pos, key_pos):
    scores = jnp.einsum(
        "qshd,kshd->qshk", query_heads, key_heads, preferred_element_type=jnp.float32
    ) * HD ** (-0.5)
    allowed = key_pos[None, :] // BLOCK <= query_pos[:, None] // BLOCK
    return (scores, allowed[:, None, None, :])


def by_blocks(step_fn, carry, pieces):
    count = pieces[0].shape[0]
    sub_width = math.gcd(count, SUB_ROWS)
    split = tuple(
        (entry.reshape((count // sub_width, sub_width) + entry.shape[1:]) for entry in pieces)
    )

    def advance(state, item):
        block_index, parts = item
        return (step_fn(state, parts, block_index * sub_width), None)

    state, unused = lax.scan(
        advance, carry, (jnp.arange(count // sub_width, dtype=jnp.int32), split)
    )
    return state


def general_device(
    inputs,
    cotangent,
    ln1_gain,
    ln1_bias,
    qkv_weight,
    qv_bias,
    proj_weight,
    proj_bias,
    ln2_gain,
    ln2_bias,
    fc_weight,
    fc_bias,
    fc2_weight,
    fc2_bias,
):
    row_count, seq_count, model_width = inputs.shape
    tokens = row_count * seq_count
    tp_count = lax.axis_size("tp")
    share_rows = row_count // tp_count
    share_tokens = share_rows * seq_count
    share_first = lax.axis_index("tp") * share_tokens

    def own_rows(values):
        return lax.dynamic_slice_in_dim(values, share_first, share_tokens, 0)

    gathered = (
        lax.all_gather(ln1_gain, "fsdp", axis=0, tiled=True),
        lax.all_gather(ln1_bias, "fsdp", axis=0, tiled=True),
        lax.all_gather(qkv_weight, "fsdp", axis=1, tiled=True),
        lax.all_gather(qv_bias, "fsdp", axis=2, tiled=True),
        lax.all_gather(proj_weight, "fsdp", axis=1, tiled=True),
        lax.all_gather(proj_bias, "fsdp", axis=0, tiled=True),
        lax.all_gather(ln2_gain, "fsdp", axis=0, tiled=True),
        lax.all_gather(ln2_bias, "fsdp", axis=0, tiled=True),
        lax.all_gather(fc_weight, "fsdp", axis=0, tiled=True),
        lax.all_gather(fc_bias, "fsdp", axis=1, tiled=True),
        lax.all_gather(fc2_weight, "fsdp", axis=1, tiled=True),
        lax.all_gather(fc2_bias, "fsdp", axis=0, tiled=True),
    )
    (
        gain_one,
        shift_one,
        qkv_full,
        bias_qv,
        proj_full,
        bias_proj,
        gain_two,
        shift_two,
        fc_full,
        bias_fc,
        fc2_full,
        bias_fc2,
    ) = gathered
    head_width = qkv_full.shape[2]
    gain_one_f = gain_one.astype(jnp.float32)
    gain_two_f = gain_two.astype(jnp.float32)
    flat = inputs.reshape(tokens, model_width).astype(jnp.float32)
    first_f, normed_one, spread_one = norm_forward(flat, gain_one_f, shift_one.astype(jnp.float32))
    first_in = first_f.astype(jnp.bfloat16)
    bias_rows = bias_qv.reshape(2, head_width).astype(jnp.float32)
    projected = jnp.einsum("td,cdf->ctf", first_in, qkv_full, preferred_element_type=jnp.float32)
    query_three = (
        (projected[0] + bias_rows[0]).astype(jnp.bfloat16).reshape(row_count, seq_count, head_width)
    )
    key_three = projected[1].astype(jnp.bfloat16).reshape(row_count, seq_count, head_width)
    value_three = (
        (projected[2] + bias_rows[1]).astype(jnp.bfloat16).reshape(row_count, seq_count, head_width)
    )
    query_heads = split_heads(query_three)
    key_heads = split_heads(key_three)
    value_heads = split_heads(value_three)
    local_heads = query_heads.shape[2]
    cycle_place = lax.axis_index("ctx")
    my_first = cycle_place * row_count
    my_pos = my_first + jnp.arange(row_count, dtype=jnp.int32)
    last_block = (my_first + row_count - 1) // BLOCK
    scale = HD ** (-0.5)

    def forward_step(state, parts, first_row):
        key_part, value_part = parts
        key_pos = first_row + jnp.arange(key_part.shape[0], dtype=jnp.int32)

        def update(inner):
            acc_sum, row_top, denom_sum = inner
            scores, allowed = block_scores(query_heads, split_heads(key_part), my_pos, key_pos)
            scores = jnp.where(allowed, scores, NEGATIVE)
            new_top = jnp.maximum(row_top, jnp.max(scores, axis=-1))
            rescale = jnp.exp(row_top - new_top)
            block_weights = jnp.where(allowed, jnp.exp(scores - new_top[..., None]), 0.0)
            denom_sum = denom_sum * rescale + jnp.sum(block_weights, axis=-1)
            acc_sum = acc_sum * rescale[..., None] + jnp.einsum(
                "qshk,kshd->qshd",
                block_weights.astype(jnp.bfloat16),
                split_heads(value_part),
                preferred_element_type=jnp.float32,
            )
            return (acc_sum, new_top, denom_sum)

        return lax.cond(first_row // BLOCK > last_block, lambda inner: inner, update, state)

    stat_shape = (row_count, seq_count, local_heads)
    start_state = (
        jnp.zeros(query_heads.shape, jnp.float32),
        jnp.full(stat_shape, NEGATIVE, jnp.float32),
        jnp.zeros(stat_shape, jnp.float32),
    )
    acc_sum, row_top, denom_sum = by_blocks(
        forward_step,
        start_state,
        (
            lax.all_gather(key_three, "ctx", axis=0, tiled=True),
            lax.all_gather(value_three, "ctx", axis=0, tiled=True),
        ),
    )
    attended_f = acc_sum / denom_sum[..., None]
    log_total = row_top + jnp.log(denom_sum)
    attended = attended_f.reshape(tokens, head_width).astype(jnp.bfloat16)
    attn_term = jnp.dot(attended, proj_full, preferred_element_type=jnp.float32)
    mixed_rows = flat + lax.psum(attn_term, "tp") + bias_proj.astype(jnp.float32)
    second_f, normed_two, spread_two = norm_forward(
        mixed_rows, gain_two_f, shift_two.astype(jnp.float32)
    )
    second_in = second_f.astype(jnp.bfloat16)
    pre_act = jnp.dot(second_in, fc_full, preferred_element_type=jnp.float32) + bias_fc.reshape(
        -1
    ).astype(jnp.float32)
    activated, gelu_pull = jax.vjp(partial(jax.nn.gelu, approximate=True), pre_act)
    hidden = activated.astype(jnp.bfloat16)
    mlp_term = jnp.dot(hidden, fc2_full, preferred_element_type=jnp.float32)
    final_share = own_rows(mixed_rows + lax.psum(mlp_term, "tp") + bias_fc2.astype(jnp.float32))
    output = final_share.astype(jnp.bfloat16).reshape(share_rows, seq_count, model_width)
    grad_rows = cotangent.reshape(tokens, model_width)
    grad_y = grad_rows.astype(jnp.float32)
    grad_bias_fc2 = jnp.sum(grad_y, axis=0)
    grad_fc2 = left_inner(hidden, grad_rows)
    hidden_grad = right_inner(grad_rows, fc2_full)
    (pre_grad_f,) = gelu_pull(hidden_grad)
    pre_grad = pre_grad_f.astype(jnp.bfloat16)
    grad_bias_fc = jnp.sum(pre_grad.astype(jnp.float32), axis=0)
    grad_fc = left_inner(second_in, pre_grad)
    second_term = right_inner(pre_grad, fc_full)
    second_grad = lax.psum(second_term, "tp")
    grad_gain_two = jnp.sum(second_grad * normed_two, axis=0)
    grad_shift_two = jnp.sum(second_grad, axis=0)
    mixed_grad = grad_y + norm_backward(second_grad, normed_two, spread_two, gain_two_f)
    branch_grad = mixed_grad.astype(jnp.bfloat16)
    grad_bias_proj = jnp.sum(branch_grad.astype(jnp.float32), axis=0)
    grad_proj = left_inner(attended, branch_grad)
    attended_grad = right_inner(branch_grad, proj_full).astype(jnp.bfloat16)
    grad_three = attended_grad.reshape(row_count, seq_count, head_width)
    grad_heads = split_heads(grad_three)
    delta_rows = jnp.sum(grad_heads.astype(jnp.float32) * attended_f, axis=-1)
    lse_all, delta_all = (
        lax.all_gather(log_total, "ctx", axis=0, tiled=True),
        lax.all_gather(delta_rows, "ctx", axis=0, tiled=True),
    )

    def back_step(state, parts, first_row):
        query_part_flat, key_part_flat, value_part_flat, grad_part_flat = parts
        count = query_part_flat.shape[0]
        other_pos = first_row + jnp.arange(count, dtype=jnp.int32)
        query_acc, key_acc, value_acc = state

        def query_update(acc_in):
            key_part = split_heads(key_part_flat)
            scores, allowed = block_scores(query_heads, key_part, my_pos, other_pos)
            attn_prob = jnp.where(allowed, jnp.exp(scores - log_total[..., None]), 0.0)
            prob_grad = jnp.einsum(
                "qshd,kshd->qshk",
                grad_heads,
                split_heads(value_part_flat),
                preferred_element_type=jnp.float32,
            )
            score_grad = (attn_prob * (prob_grad - delta_rows[..., None])).astype(jnp.bfloat16)
            return (
                acc_in
                + jnp.einsum(
                    "qshk,kshd->qshd", score_grad, key_part, preferred_element_type=jnp.float32
                )
                * scale
            )

        def key_update(inner):
            key_in, value_in = inner
            lse_part = lax.dynamic_slice_in_dim(lse_all, first_row, count, 0)
            delta_part = lax.dynamic_slice_in_dim(delta_all, first_row, count, 0)
            query_part = split_heads(query_part_flat)
            grad_part = split_heads(grad_part_flat)
            scores, allowed = block_scores(query_part, key_heads, other_pos, my_pos)
            attn_prob = jnp.where(allowed, jnp.exp(scores - lse_part[..., None]), 0.0)
            prob_grad = jnp.einsum(
                "qshd,kshd->qshk", grad_part, value_heads, preferred_element_type=jnp.float32
            )
            score_grad = (attn_prob * (prob_grad - delta_part[..., None])).astype(jnp.bfloat16)
            key_in = (
                key_in
                + jnp.einsum(
                    "qshk,qshd->kshd", score_grad, query_part, preferred_element_type=jnp.float32
                )
                * scale
            )
            value_in = value_in + jnp.einsum(
                "qshk,qshd->kshd",
                attn_prob.astype(jnp.bfloat16),
                grad_part,
                preferred_element_type=jnp.float32,
            )
            return (key_in, value_in)

        query_acc = lax.cond(
            first_row // BLOCK > last_block, lambda acc_in: acc_in, query_update, query_acc
        )
        key_acc, value_acc = lax.cond(
            my_first // BLOCK > (first_row + count - 1) // BLOCK,
            lambda inner: inner,
            key_update,
            (key_acc, value_acc),
        )
        return (query_acc, key_acc, value_acc)

    zero_heads = jnp.zeros(query_heads.shape, jnp.float32)
    query_grad_f, key_grad_f, value_grad_f = by_blocks(
        back_step,
        (zero_heads, zero_heads, zero_heads),
        (
            lax.all_gather(query_three, "ctx", axis=0, tiled=True),
            lax.all_gather(key_three, "ctx", axis=0, tiled=True),
            lax.all_gather(value_three, "ctx", axis=0, tiled=True),
            lax.all_gather(grad_three, "ctx", axis=0, tiled=True),
        ),
    )
    query_grad = query_grad_f.reshape(tokens, head_width).astype(jnp.bfloat16)
    key_grad = key_grad_f.reshape(tokens, head_width).astype(jnp.bfloat16)
    value_grad = value_grad_f.reshape(tokens, head_width).astype(jnp.bfloat16)
    stacked_grad = jnp.stack([query_grad, key_grad, value_grad])
    grad_bias_qv = jnp.stack(
        [
            jnp.sum(query_grad.astype(jnp.float32), axis=0),
            jnp.sum(value_grad.astype(jnp.float32), axis=0),
        ]
    ).reshape(bias_qv.shape)
    grad_qkv = jnp.einsum("td,ctf->cdf", first_in, stacked_grad, preferred_element_type=jnp.float32)
    first_term = jnp.einsum(
        "ctf,cdf->td", stacked_grad, qkv_full, preferred_element_type=jnp.float32
    )
    first_grad = lax.psum(first_term, "tp")
    grad_gain_one = jnp.sum(first_grad * normed_one, axis=0)
    grad_shift_one = jnp.sum(first_grad, axis=0)
    input_rows = own_rows(
        mixed_grad + norm_backward(first_grad, normed_one, spread_one, gain_one_f)
    )
    input_grad = input_rows.astype(jnp.bfloat16).reshape(share_rows, seq_count, model_width)
    shares = (
        lax.psum_scatter(grad_gain_one, ("fsdp", "ctx"), scatter_dimension=0, tiled=True),
        lax.psum_scatter(grad_shift_one, ("fsdp", "ctx"), scatter_dimension=0, tiled=True),
        lax.psum_scatter(grad_qkv, ("fsdp", "ctx"), scatter_dimension=1, tiled=True),
        lax.psum_scatter(grad_bias_qv, ("fsdp", "ctx"), scatter_dimension=2, tiled=True),
        lax.psum_scatter(grad_proj, ("fsdp", "ctx"), scatter_dimension=1, tiled=True),
        lax.psum_scatter(grad_bias_proj, ("fsdp", "ctx"), scatter_dimension=0, tiled=True),
        lax.psum_scatter(grad_gain_two, ("fsdp", "ctx"), scatter_dimension=0, tiled=True),
        lax.psum_scatter(grad_shift_two, ("fsdp", "ctx"), scatter_dimension=0, tiled=True),
        lax.psum_scatter(grad_fc, ("fsdp", "ctx"), scatter_dimension=0, tiled=True),
        lax.psum_scatter(
            grad_bias_fc.reshape(bias_fc.shape), ("fsdp", "ctx"), scatter_dimension=1, tiled=True
        ),
        lax.psum_scatter(grad_fc2, ("fsdp", "ctx"), scatter_dimension=1, tiled=True),
        lax.psum_scatter(grad_bias_fc2, ("fsdp", "ctx"), scatter_dimension=0, tiled=True),
    )
    summed = (
        lax.all_gather(shares[0], "ctx", axis=0, tiled=True),
        lax.all_gather(shares[1], "ctx", axis=0, tiled=True),
        lax.all_gather(shares[2], "ctx", axis=1, tiled=True),
        lax.all_gather(shares[3], "ctx", axis=2, tiled=True),
        lax.all_gather(shares[4], "ctx", axis=1, tiled=True),
        lax.all_gather(shares[5], "ctx", axis=0, tiled=True),
        lax.all_gather(shares[6], "ctx", axis=0, tiled=True),
        lax.all_gather(shares[7], "ctx", axis=0, tiled=True),
        lax.all_gather(shares[8], "ctx", axis=0, tiled=True),
        lax.all_gather(shares[9], "ctx", axis=1, tiled=True),
        lax.all_gather(shares[10], "ctx", axis=1, tiled=True),
        lax.all_gather(shares[11], "ctx", axis=0, tiled=True),
    )
    return (
        output,
        input_grad,
        summed[0],
        summed[1],
        summed[2],
        summed[3],
        summed[4],
        summed[5],
        summed[6],
        summed[7],
        summed[8],
        summed[9],
        summed[10],
        summed[11],
    )


SWAP = ((0, 1), (1, 0))
MATE = ((0, 1), (1, 0), (2, 3), (3, 2))
PEER = ((0, 2), (2, 0), (1, 3), (3, 1))
INWARD = ((0, 1), (3, 2))
MIDDLE = ((1, 2), (2, 1))
OUTWARD = ((1, 0), (2, 3))


def xor_pairs(count, mask):
    return tuple((place, place ^ mask) for place in range(count))


def bf(values):
    return values.astype(jnp.bfloat16)


def f32(values):
    return values.astype(jnp.float32)


def matmul(left, right):
    return jnp.dot(left, right, preferred_element_type=jnp.float32)


def contract(left, right, left_dim, right_dim):
    return lax.dot_general(
        left,
        right,
        (((left_dim,), (right_dim,)), ((), ())),
        preferred_element_type=jnp.float32,
    )


def merged(values):
    return values.reshape(-1, values.shape[-1])


def stack_heads(values):
    heads = values.shape[-1] // HD
    lane_head = lax.broadcasted_iota(jnp.int32, values.shape, 1) // HD
    blank = jnp.zeros_like(values)
    return jnp.concatenate(
        [jnp.where(lane_head == head, values, blank) for head in range(heads)], axis=0
    )


def attend_kernel(query_ref, key_ref, value_ref, out_ref, lse_ref, score_ref, acc_ref):
    block = pl.program_id(0)
    query = merged(query_ref[:, 0])
    rows, width = query.shape
    heads = width // HD
    scale = HD ** (-0.5)

    def score(other, top):
        values = contract(stack_heads(merged(key_ref[:, other])), query, 1, 1)
        values = values.reshape(heads, rows, rows)
        score_ref[other] = values
        return jnp.maximum(top, jnp.max(values, axis=1, keepdims=True))

    top = lax.fori_loop(0, block + 1, score, jnp.full((heads, 1, rows), NEGATIVE, jnp.float32))

    def weigh(other, total):
        values = jnp.exp((score_ref[other] - top) * scale)
        score_ref[other] = values
        return total + jnp.sum(values, axis=1, keepdims=True)

    total = lax.fori_loop(0, block + 1, weigh, jnp.zeros((heads, 1, rows), jnp.float32))
    lse_ref[0] = top * scale + jnp.log(total)
    inverse = 1.0 / total
    acc_ref[...] = jnp.zeros_like(acc_ref)

    def mix(other, unused):
        prob = bf(score_ref[other] * inverse).reshape(heads * rows, rows)
        acc_ref[...] += contract(prob, stack_heads(merged(value_ref[:, other])), 0, 0)
        return unused

    lax.fori_loop(0, block + 1, mix, 0)
    out_ref[:, 0] = bf(acc_ref[...]).reshape(out_ref.shape[0], out_ref.shape[2], width)


def attend_back_kernel(
    query_ref,
    key_ref,
    value_ref,
    out_ref,
    grad_ref,
    lse_ref,
    query_grad_ref,
    key_grad_ref,
    value_grad_ref,
    query_acc,
    key_acc,
    value_acc,
    query_stack,
    grad_stack,
):
    block = pl.program_id(0)
    blocks = pl.num_programs(0)
    query = merged(query_ref[:, 0])
    grad = merged(grad_ref[:, 0])
    rows, width = query.shape
    heads = width // HD
    lane_head = lax.broadcasted_iota(jnp.int32, (rows, width), 1) // HD
    scale = HD ** (-0.5)
    query_stack[...] = stack_heads(query)
    grad_stack[...] = stack_heads(grad)
    products = f32(grad) * f32(merged(out_ref[:, 0]))
    deltas = []
    for head in range(heads):
        column = jnp.sum(jnp.where(lane_head == head, products, 0.0), axis=1, keepdims=True)
        deltas.append(jnp.transpose(jnp.broadcast_to(column, (rows, 128)))[0:1])
    delta = jnp.concatenate(deltas, axis=1)
    lse = jnp.concatenate([lse_ref[0, head] for head in range(heads)], axis=1)
    query_acc[...] = jnp.zeros_like(query_acc)

    @pl.when(block == 0)
    def clear():
        key_acc[...] = jnp.zeros_like(key_acc)
        value_acc[...] = jnp.zeros_like(value_acc)

    def one_block(other, unused):
        key = merged(key_ref[:, other])
        scores = contract(key, query_stack[...], 1, 1)
        prob_grad = contract(merged(value_ref[:, other]), grad_stack[...], 1, 1)
        prob = jnp.exp(scores * scale - lse)
        score_grad = bf(prob * (prob_grad - delta))
        value_acc[other] += contract(bf(prob), grad_stack[...], 1, 0)
        key_acc[other] += contract(score_grad, query_stack[...], 1, 0)
        tall = jnp.concatenate(
            [score_grad[:, head * rows : (head + 1) * rows] for head in range(heads)], axis=0
        )
        query_acc[...] += contract(tall, stack_heads(key), 0, 0)
        return unused

    lax.fori_loop(0, block + 1, one_block, 0)
    shape = (query_grad_ref.shape[0], query_grad_ref.shape[2], width)
    query_grad_ref[:, 0] = bf(query_acc[...] * scale).reshape(shape)

    @pl.when(block == blocks - 1)
    def finish():
        for other in range(key_acc.shape[0]):
            key_grad_ref[:, other] = bf(key_acc[other] * scale).reshape(shape)
            value_grad_ref[:, other] = bf(value_acc[other]).reshape(shape)


def attend(query, key, value):
    slots, blocks, part, width = query.shape
    rows = slots * part
    heads = width // HD
    one = pl.BlockSpec((slots, 1, part, width), lambda i: (0, i, 0, 0))
    whole = pl.BlockSpec((slots, blocks, part, width), lambda i: (0, 0, 0, 0))
    pairs = blocks * (blocks + 1) // 2 * heads
    return pl.pallas_call(
        attend_kernel,
        grid=(blocks,),
        in_specs=[one, whole, whole],
        out_specs=[one, pl.BlockSpec((1, heads, 1, rows), lambda i: (i, 0, 0, 0))],
        out_shape=[
            jax.ShapeDtypeStruct(query.shape, jnp.bfloat16),
            jax.ShapeDtypeStruct((blocks, heads, 1, rows), jnp.float32),
        ],
        scratch_shapes=[
            pltpu.VMEM((blocks, heads, rows, rows), jnp.float32),
            pltpu.VMEM((rows, width), jnp.float32),
        ],
        cost_estimate=pl.CostEstimate(
            flops=pairs * 4 * rows * rows * width,
            bytes_accessed=4 * query.size * 2,
            transcendentals=pairs * rows * rows,
        ),
        name="attend",
    )(query, key, value)


def attend_back(query, key, value, out, grad, lse):
    slots, blocks, part, width = query.shape
    rows = slots * part
    heads = width // HD
    one = pl.BlockSpec((slots, 1, part, width), lambda i: (0, i, 0, 0))
    whole = pl.BlockSpec((slots, blocks, part, width), lambda i: (0, 0, 0, 0))
    pairs = blocks * (blocks + 1) // 2 * heads
    return pl.pallas_call(
        attend_back_kernel,
        grid=(blocks,),
        in_specs=[
            one,
            whole,
            whole,
            one,
            one,
            pl.BlockSpec((1, heads, 1, rows), lambda i: (i, 0, 0, 0)),
        ],
        out_specs=[one, whole, whole],
        out_shape=[jax.ShapeDtypeStruct(query.shape, jnp.bfloat16)] * 3,
        scratch_shapes=[
            pltpu.VMEM((rows, width), jnp.float32),
            pltpu.VMEM((blocks, rows, width), jnp.float32),
            pltpu.VMEM((blocks, rows, width), jnp.float32),
            pltpu.VMEM((heads * rows, width), jnp.bfloat16),
            pltpu.VMEM((heads * rows, width), jnp.bfloat16),
        ],
        cost_estimate=pl.CostEstimate(
            flops=pairs * 10 * rows * rows * width,
            bytes_accessed=8 * query.size * 2,
            transcendentals=pairs * rows * rows,
        ),
        name="attend_back",
    )(query, key, value, out, grad, lse)


def spread_parts(values):
    mate = lax.ppermute(values, "tp", MATE)
    peer = lax.ppermute(values, "tp", PEER)
    across = lax.ppermute(peer, "tp", MATE)
    return (values, mate, peer, across)


def spread_rows(values):
    return jnp.concatenate(spread_parts(values), axis=0)


def gather_sum(part_of):
    across = lax.ppermute(bf(part_of(3)), "tp", MATE)
    peer = lax.ppermute(bf(part_of(2) + f32(across)), "tp", PEER)
    mate = lax.ppermute(bf(part_of(1)), "tp", MATE)
    return part_of(0) + f32(mate) + f32(peer)


def sum_weight(kept, sent):
    half = kept + f32(lax.ppermute(bf(sent), "fsdp", SWAP))
    pair = bf(half + f32(lax.ppermute(bf(half), "ctx", INWARD)))
    total = bf(f32(pair) + f32(lax.ppermute(pair, "ctx", MIDDLE)))
    outer = lax.ppermute(total, "ctx", OUTWARD)
    place = lax.axis_index("ctx")
    inner = jnp.logical_and(place > 0, place < 3)
    return f32(jnp.where(inner, total, outer))


def fast_device(
    inputs,
    cotangent,
    ln1_gain,
    ln1_bias,
    qkv_weight,
    qv_bias,
    proj_weight,
    proj_bias,
    ln2_gain,
    ln2_bias,
    fc_weight,
    fc_bias,
    fc2_weight,
    fc2_bias,
):
    row_count, seq_count, width = inputs.shape
    tp_count = lax.axis_size("tp")
    ctx_count = lax.axis_size("ctx")
    share_rows = row_count // tp_count
    share_tokens = share_rows * ctx_count
    place_f = lax.axis_index("fsdp")
    place_c = lax.axis_index("ctx")
    place_t = lax.axis_index("tp")
    half = width // 2
    lower = place_f == 0

    def own_first(values):
        flipped = jnp.concatenate([values[..., half:], values[..., :half]], axis=-1)
        return jnp.where(lower, values, flipped)

    def join(own, other, axis):
        return jnp.where(
            lower,
            jnp.concatenate([own, other], axis=axis),
            jnp.concatenate([other, own], axis=axis),
        )

    def to_sequences(values):
        mine = lax.dynamic_slice_in_dim(values, place_t * share_rows, share_rows, 0)
        mine = own_first(mine)
        got = []
        for step in range(ctx_count):
            piece = lax.dynamic_index_in_dim(mine, place_c ^ step, 1, keepdims=False)
            if step:
                piece = lax.ppermute(piece, "ctx", xor_pairs(ctx_count, step))
            got.append(piece)
        stacked = jnp.stack(got)
        ordered = [
            lax.dynamic_index_in_dim(stacked, place_c ^ step, 0, keepdims=False)
            for step in range(ctx_count)
        ]
        return jnp.concatenate(ordered, axis=0)

    def to_positions(values):
        mine = own_first(values).reshape(ctx_count, share_rows, width)
        got = []
        for step in range(ctx_count):
            piece = lax.dynamic_index_in_dim(mine, place_c ^ step, 0, keepdims=False)
            if step:
                piece = lax.ppermute(piece, "ctx", xor_pairs(ctx_count, step))
            got.append(piece)
        stacked = jnp.stack(got)
        ordered = [
            lax.dynamic_index_in_dim(stacked, place_c ^ step, 0, keepdims=False)
            for step in range(ctx_count)
        ]
        return jnp.stack(ordered, axis=1)

    flat = f32(to_sequences(inputs))

    small_own = jnp.concatenate(
        [
            jnp.stack([ln1_gain, ln1_bias, proj_bias, ln2_gain, ln2_bias, fc2_bias]).reshape(-1),
            qv_bias.reshape(-1),
            fc_bias.reshape(-1),
        ]
    ).reshape(-1, 128)
    small_other = lax.ppermute(small_own, "fsdp", SWAP)
    qkv_other = lax.ppermute(qkv_weight, "fsdp", SWAP)
    proj_other = lax.ppermute(proj_weight, "fsdp", SWAP)
    fc_other = lax.ppermute(fc_weight, "fsdp", SWAP)
    fc2_other = lax.ppermute(fc2_weight, "fsdp", SWAP)
    qkv_full = jnp.concatenate([qkv_weight, qkv_other], axis=1)
    proj_full = jnp.concatenate([proj_weight, proj_other], axis=1)
    fc_full = jnp.concatenate([fc_weight, fc_other], axis=0)
    fc2_full = jnp.concatenate([fc2_weight, fc2_other], axis=1)

    small_own = small_own.reshape(-1)
    small_other = small_other.reshape(-1)
    vectors = f32(
        jnp.concatenate(
            [small_own[: 6 * half].reshape(6, half), small_other[: 6 * half].reshape(6, half)],
            axis=1,
        )
    )
    gain_one, shift_one, bias_proj, gain_two, shift_two, bias_fc2 = (vectors[n] for n in range(6))
    qv_end = 6 * half + qv_bias.size
    bias_qv = f32(
        join(
            small_own[6 * half : qv_end].reshape(qv_bias.shape),
            small_other[6 * half : qv_end].reshape(qv_bias.shape),
            2,
        )
    )
    bias_fc = f32(
        join(
            small_own[qv_end:].reshape(fc_bias.shape),
            small_other[qv_end:].reshape(fc_bias.shape),
            1,
        )
    )
    head_width = qkv_full.shape[2]
    bias_rows = bias_qv.reshape(2, head_width)

    first_f, normed_one, spread_one = norm_forward(flat, gain_one, shift_one)
    first_in = spread_rows(bf(first_f))
    head_shape = (tp_count, ctx_count, share_rows, head_width)
    query = bf(matmul(first_in, qkv_full[0]) + bias_rows[0]).reshape(head_shape)
    key = bf(matmul(first_in, qkv_full[1])).reshape(head_shape)
    value = bf(matmul(first_in, qkv_full[2]) + bias_rows[1]).reshape(head_shape)
    attended_four, lse = attend(query, key, value)
    attended = attended_four.reshape(-1, head_width)

    def rows_of(values, slot):
        return values[slot * share_tokens : (slot + 1) * share_tokens]

    attn_sum = gather_sum(lambda slot: matmul(rows_of(attended, slot), proj_full))
    mixed = flat + attn_sum + bias_proj
    second_f, normed_two, spread_two = norm_forward(mixed, gain_two, shift_two)
    second_in = spread_rows(bf(second_f))

    grad_own = to_sequences(cotangent)
    grad_rows = spread_rows(grad_own)
    grad_y = f32(grad_own)

    hidden_grad = contract(grad_rows, fc2_full, 1, 1)
    pre_act = matmul(second_in, fc_full) + bias_fc.reshape(-1)
    activated, gelu_pull = jax.vjp(partial(jax.nn.gelu, approximate=True), pre_act)
    hidden = bf(activated)
    (pre_grad_f,) = gelu_pull(hidden_grad)
    pre_grad = bf(pre_grad_f)

    second_grad = gather_sum(lambda slot: contract(rows_of(pre_grad, slot), fc_full, 1, 1))
    mixed_grad = grad_y + norm_backward(second_grad, normed_two, spread_two, gain_two)
    branch_own = bf(mixed_grad)
    branch = spread_rows(branch_own)

    mlp_sum = gather_sum(lambda slot: matmul(rows_of(hidden, slot), fc2_full))
    output = to_positions(bf(mixed + mlp_sum + bias_fc2))

    grad_fc2 = sum_weight(
        contract(hidden, grad_rows[:, :half], 0, 0), contract(hidden, grad_rows[:, half:], 0, 0)
    )
    grad_fc = sum_weight(
        contract(second_in[:, :half], pre_grad, 0, 0),
        contract(second_in[:, half:], pre_grad, 0, 0),
    )

    attended_grad = bf(contract(branch, proj_full, 1, 1)).reshape(head_shape)
    query_grad, key_grad, value_grad = (
        entry.reshape(-1, head_width)
        for entry in attend_back(query, key, value, attended_four, attended_grad, lse)
    )
    grad_proj = sum_weight(
        contract(attended, branch[:, :half], 0, 0), contract(attended, branch[:, half:], 0, 0)
    )

    def first_part(slot):
        return (
            contract(rows_of(query_grad, slot), qkv_full[0], 1, 1)
            + contract(rows_of(key_grad, slot), qkv_full[1], 1, 1)
            + contract(rows_of(value_grad, slot), qkv_full[2], 1, 1)
        )

    first_grad = gather_sum(first_part)
    input_own = mixed_grad + norm_backward(first_grad, normed_one, spread_one, gain_one)
    input_grad = to_positions(bf(input_own))

    def qkv_grads(columns):
        return jnp.stack(
            [contract(columns, entry, 0, 0) for entry in (query_grad, key_grad, value_grad)]
        )

    grad_qkv = sum_weight(qkv_grads(first_in[:, :half]), qkv_grads(first_in[:, half:]))

    token_sums = jnp.stack(
        [
            jnp.sum(first_grad * normed_one, axis=0),
            jnp.sum(first_grad, axis=0),
            jnp.sum(f32(branch_own), axis=0),
            jnp.sum(second_grad * normed_two, axis=0),
            jnp.sum(second_grad, axis=0),
            jnp.sum(grad_y, axis=0),
        ]
    )
    sum_qv = jnp.stack(
        [jnp.sum(f32(query_grad), axis=0), jnp.sum(f32(value_grad), axis=0)]
    ).reshape(bias_qv.shape)
    sum_fc = jnp.sum(f32(pre_grad), axis=0).reshape(bias_fc.shape)
    qv_part = qv_bias.shape[2]
    fc_part = fc_bias.shape[1]

    def small_pack(vector_half, which):
        return jnp.concatenate(
            [
                vector_half.reshape(-1),
                lax.dynamic_slice_in_dim(sum_qv, which * qv_part, qv_part, 2).reshape(-1),
                lax.dynamic_slice_in_dim(sum_fc, which * fc_part, fc_part, 1).reshape(-1),
            ]
        ).reshape(-1, 128)

    small = small_pack(token_sums[:, :half], place_f) + lax.ppermute(
        small_pack(token_sums[:, half:], 1 - place_f), "fsdp", SWAP
    )
    split = 6 * half // 128
    small_d = small[:split]
    small_d = small_d + lax.ppermute(small_d, "tp", MATE)
    small_d = small_d + lax.ppermute(small_d, "tp", PEER)
    small = jnp.concatenate([small_d, small[split:]], axis=0)
    small = small + lax.ppermute(small, "ctx", xor_pairs(ctx_count, 1))
    small = small + lax.ppermute(small, "ctx", xor_pairs(ctx_count, 2))
    small = small.reshape(-1)
    sums = small[: 6 * half].reshape(6, half)
    return (
        output,
        input_grad,
        sums[0],
        sums[1],
        grad_qkv,
        small[6 * half : qv_end].reshape(qv_bias.shape),
        grad_proj,
        sums[2],
        sums[3],
        sums[4],
        grad_fc,
        small[qv_end:].reshape(fc_bias.shape),
        grad_fc2,
        sums[5],
    )


def on_device(*args):
    rows, sequences, unused_width = args[0].shape
    whole_sequences = (
        lax.axis_size("fsdp") == 2
        and lax.axis_size("tp") == 4
        and lax.axis_size("ctx") == 4
        and sequences == 4
        and rows == BLOCK
    )
    return (fast_device if whole_sequences else general_device)(*args)


def solution(mesh):
    return jax.shard_map(
        on_device,
        mesh=mesh,
        in_specs=(
            P("ctx", "fsdp", None),
            P("ctx", "fsdp", None),
            P("fsdp"),
            P("fsdp"),
            P(None, "fsdp", "tp"),
            P(None, "tp", "fsdp"),
            P("tp", "fsdp"),
            P("fsdp"),
            P("fsdp"),
            P("fsdp"),
            P("fsdp", "tp"),
            P("tp", "fsdp"),
            P("tp", "fsdp"),
            P("fsdp"),
        ),
        out_specs=(
            P(("ctx", "tp"), "fsdp", None),
            P(("ctx", "tp"), "fsdp", None),
            P("fsdp"),
            P("fsdp"),
            P(None, "fsdp", "tp"),
            P(None, "tp", "fsdp"),
            P("tp", "fsdp"),
            P("fsdp"),
            P("fsdp"),
            P("fsdp"),
            P("fsdp", "tp"),
            P("tp", "fsdp"),
            P("tp", "fsdp"),
            P("fsdp"),
        ),
        check_vma=False,
    )
```

```python
from functools import partial
import math

import jax
import jax.numpy as jnp
from jax import lax
from jax.experimental import pallas as pl
from jax.experimental.pallas import tpu as pltpu
from jax.sharding import PartitionSpec as P


HD = 64
BLOCK = 256


EPSILON = 1e-05
NEGATIVE = -1e30
SUB_ROWS = 512


def norm_forward(values, gain, shift):
    centred = values - jnp.mean(values, axis=-1, keepdims=True)
    spread = lax.rsqrt(jnp.mean(centred * centred, axis=-1, keepdims=True) + EPSILON)
    normed = centred * spread
    return (normed * gain + shift, normed, spread)


def norm_backward(grad_out, normed, spread, gain):
    scaled = grad_out * gain
    return spread * (
        scaled
        - jnp.mean(scaled, axis=-1, keepdims=True)
        - normed * jnp.mean(scaled * normed, axis=-1, keepdims=True)
    )


def left_inner(left, right):
    return lax.dot_general(
        left, right, (((0,), (0,)), ((), ())), preferred_element_type=jnp.float32
    )


def right_inner(left, right):
    return lax.dot_general(
        left, right, (((1,), (1,)), ((), ())), preferred_element_type=jnp.float32
    )


def split_heads(values):
    return values.reshape(values.shape[0], values.shape[1], -1, HD)


def block_scores(query_heads, key_heads, query_pos, key_pos):
    scores = jnp.einsum(
        "qshd,kshd->qshk", query_heads, key_heads, preferred_element_type=jnp.float32
    ) * HD ** (-0.5)
    allowed = key_pos[None, :] // BLOCK <= query_pos[:, None] // BLOCK
    return (scores, allowed[:, None, None, :])


def by_blocks(step_fn, carry, pieces):
    count = pieces[0].shape[0]
    sub_width = math.gcd(count, SUB_ROWS)
    split = tuple(
        (entry.reshape((count // sub_width, sub_width) + entry.shape[1:]) for entry in pieces)
    )

    def advance(state, item):
        block_index, parts = item
        return (step_fn(state, parts, block_index * sub_width), None)

    state, _ = lax.scan(advance, carry, (jnp.arange(count // sub_width, dtype=jnp.int32), split))
    return state


def general_device(
    inputs,
    cotangent,
    ln1_gain,
    ln1_bias,
    qkv_weight,
    qv_bias,
    proj_weight,
    proj_bias,
    ln2_gain,
    ln2_bias,
    fc_weight,
    fc_bias,
    fc2_weight,
    fc2_bias,
):
    row_count, seq_count, model_width = inputs.shape
    tokens = row_count * seq_count
    tp_count = lax.axis_size("tp")
    share_rows = row_count // tp_count
    share_tokens = share_rows * seq_count
    share_first = lax.axis_index("tp") * share_tokens

    def own_rows(values):
        return lax.dynamic_slice_in_dim(values, share_first, share_tokens, 0)

    gathered = (
        lax.all_gather(ln1_gain, "fsdp", axis=0, tiled=True),
        lax.all_gather(ln1_bias, "fsdp", axis=0, tiled=True),
        lax.all_gather(qkv_weight, "fsdp", axis=1, tiled=True),
        lax.all_gather(qv_bias, "fsdp", axis=2, tiled=True),
        lax.all_gather(proj_weight, "fsdp", axis=1, tiled=True),
        lax.all_gather(proj_bias, "fsdp", axis=0, tiled=True),
        lax.all_gather(ln2_gain, "fsdp", axis=0, tiled=True),
        lax.all_gather(ln2_bias, "fsdp", axis=0, tiled=True),
        lax.all_gather(fc_weight, "fsdp", axis=0, tiled=True),
        lax.all_gather(fc_bias, "fsdp", axis=1, tiled=True),
        lax.all_gather(fc2_weight, "fsdp", axis=1, tiled=True),
        lax.all_gather(fc2_bias, "fsdp", axis=0, tiled=True),
    )
    (
        gain_one,
        shift_one,
        qkv_full,
        bias_qv,
        proj_full,
        bias_proj,
        gain_two,
        shift_two,
        fc_full,
        bias_fc,
        fc2_full,
        bias_fc2,
    ) = gathered
    head_width = qkv_full.shape[2]
    gain_one_f = gain_one.astype(jnp.float32)
    gain_two_f = gain_two.astype(jnp.float32)
    flat = inputs.reshape(tokens, model_width).astype(jnp.float32)
    first_f, normed_one, spread_one = norm_forward(flat, gain_one_f, shift_one.astype(jnp.float32))
    first_in = first_f.astype(jnp.bfloat16)
    bias_rows = bias_qv.reshape(2, head_width).astype(jnp.float32)
    projected = jnp.einsum("td,cdf->ctf", first_in, qkv_full, preferred_element_type=jnp.float32)
    query_three = (
        (projected[0] + bias_rows[0]).astype(jnp.bfloat16).reshape(row_count, seq_count, head_width)
    )
    key_three = projected[1].astype(jnp.bfloat16).reshape(row_count, seq_count, head_width)
    value_three = (
        (projected[2] + bias_rows[1]).astype(jnp.bfloat16).reshape(row_count, seq_count, head_width)
    )
    query_heads = split_heads(query_three)
    key_heads = split_heads(key_three)
    value_heads = split_heads(value_three)
    local_heads = query_heads.shape[2]
    cycle_place = lax.axis_index("ctx")
    my_first = cycle_place * row_count
    my_pos = my_first + jnp.arange(row_count, dtype=jnp.int32)
    last_block = (my_first + row_count - 1) // BLOCK
    scale = HD ** (-0.5)

    def forward_step(state, parts, first_row):
        key_part, value_part = parts
        key_pos = first_row + jnp.arange(key_part.shape[0], dtype=jnp.int32)

        def update(inner):
            acc_sum, row_top, denom_sum = inner
            scores, allowed = block_scores(query_heads, split_heads(key_part), my_pos, key_pos)
            scores = jnp.where(allowed, scores, NEGATIVE)
            new_top = jnp.maximum(row_top, jnp.max(scores, axis=-1))
            rescale = jnp.exp(row_top - new_top)
            block_weights = jnp.where(allowed, jnp.exp(scores - new_top[..., None]), 0.0)
            denom_sum = denom_sum * rescale + jnp.sum(block_weights, axis=-1)
            acc_sum = acc_sum * rescale[..., None] + jnp.einsum(
                "qshk,kshd->qshd",
                block_weights.astype(jnp.bfloat16),
                split_heads(value_part),
                preferred_element_type=jnp.float32,
            )
            return (acc_sum, new_top, denom_sum)

        return lax.cond(first_row // BLOCK > last_block, lambda inner: inner, update, state)

    stat_shape = (row_count, seq_count, local_heads)
    start_state = (
        jnp.zeros(query_heads.shape, jnp.float32),
        jnp.full(stat_shape, NEGATIVE, jnp.float32),
        jnp.zeros(stat_shape, jnp.float32),
    )
    acc_sum, row_top, denom_sum = by_blocks(
        forward_step,
        start_state,
        (
            lax.all_gather(key_three, "ctx", axis=0, tiled=True),
            lax.all_gather(value_three, "ctx", axis=0, tiled=True),
        ),
    )
    attended_f = acc_sum / denom_sum[..., None]
    log_total = row_top + jnp.log(denom_sum)
    attended = attended_f.reshape(tokens, head_width).astype(jnp.bfloat16)
    attn_term = jnp.dot(attended, proj_full, preferred_element_type=jnp.float32)
    mixed_rows = flat + lax.psum(attn_term, "tp") + bias_proj.astype(jnp.float32)
    second_f, normed_two, spread_two = norm_forward(
        mixed_rows, gain_two_f, shift_two.astype(jnp.float32)
    )
    second_in = second_f.astype(jnp.bfloat16)
    pre_act = jnp.dot(second_in, fc_full, preferred_element_type=jnp.float32) + bias_fc.reshape(
        -1
    ).astype(jnp.float32)
    activated, gelu_pull = jax.vjp(partial(jax.nn.gelu, approximate=True), pre_act)
    hidden = activated.astype(jnp.bfloat16)
    mlp_term = jnp.dot(hidden, fc2_full, preferred_element_type=jnp.float32)
    final_share = own_rows(mixed_rows + lax.psum(mlp_term, "tp") + bias_fc2.astype(jnp.float32))
    output = final_share.astype(jnp.bfloat16).reshape(share_rows, seq_count, model_width)
    grad_rows = cotangent.reshape(tokens, model_width)
    grad_y = grad_rows.astype(jnp.float32)
    grad_bias_fc2 = jnp.sum(grad_y, axis=0)
    grad_fc2 = left_inner(hidden, grad_rows)
    hidden_grad = right_inner(grad_rows, fc2_full)
    (pre_grad_f,) = gelu_pull(hidden_grad)
    pre_grad = pre_grad_f.astype(jnp.bfloat16)
    grad_bias_fc = jnp.sum(pre_grad.astype(jnp.float32), axis=0)
    grad_fc = left_inner(second_in, pre_grad)
    second_term = right_inner(pre_grad, fc_full)
    second_grad = lax.psum(second_term, "tp")
    grad_gain_two = jnp.sum(second_grad * normed_two, axis=0)
    grad_shift_two = jnp.sum(second_grad, axis=0)
    mixed_grad = grad_y + norm_backward(second_grad, normed_two, spread_two, gain_two_f)
    branch_grad = mixed_grad.astype(jnp.bfloat16)
    grad_bias_proj = jnp.sum(branch_grad.astype(jnp.float32), axis=0)
    grad_proj = left_inner(attended, branch_grad)
    attended_grad = right_inner(branch_grad, proj_full).astype(jnp.bfloat16)
    grad_three = attended_grad.reshape(row_count, seq_count, head_width)
    grad_heads = split_heads(grad_three)
    delta_rows = jnp.sum(grad_heads.astype(jnp.float32) * attended_f, axis=-1)
    lse_all, delta_all = (
        lax.all_gather(log_total, "ctx", axis=0, tiled=True),
        lax.all_gather(delta_rows, "ctx", axis=0, tiled=True),
    )

    def back_step(state, parts, first_row):
        query_part_flat, key_part_flat, value_part_flat, grad_part_flat = parts
        count = query_part_flat.shape[0]
        other_pos = first_row + jnp.arange(count, dtype=jnp.int32)
        query_acc, key_acc, value_acc = state

        def query_update(acc_in):
            key_part = split_heads(key_part_flat)
            scores, allowed = block_scores(query_heads, key_part, my_pos, other_pos)
            attn_prob = jnp.where(allowed, jnp.exp(scores - log_total[..., None]), 0.0)
            prob_grad = jnp.einsum(
                "qshd,kshd->qshk",
                grad_heads,
                split_heads(value_part_flat),
                preferred_element_type=jnp.float32,
            )
            score_grad = (attn_prob * (prob_grad - delta_rows[..., None])).astype(jnp.bfloat16)
            return (
                acc_in
                + jnp.einsum(
                    "qshk,kshd->qshd", score_grad, key_part, preferred_element_type=jnp.float32
                )
                * scale
            )

        def key_update(inner):
            key_in, value_in = inner
            lse_part = lax.dynamic_slice_in_dim(lse_all, first_row, count, 0)
            delta_part = lax.dynamic_slice_in_dim(delta_all, first_row, count, 0)
            query_part = split_heads(query_part_flat)
            grad_part = split_heads(grad_part_flat)
            scores, allowed = block_scores(query_part, key_heads, other_pos, my_pos)
            attn_prob = jnp.where(allowed, jnp.exp(scores - lse_part[..., None]), 0.0)
            prob_grad = jnp.einsum(
                "qshd,kshd->qshk", grad_part, value_heads, preferred_element_type=jnp.float32
            )
            score_grad = (attn_prob * (prob_grad - delta_part[..., None])).astype(jnp.bfloat16)
            key_in = (
                key_in
                + jnp.einsum(
                    "qshk,qshd->kshd", score_grad, query_part, preferred_element_type=jnp.float32
                )
                * scale
            )
            value_in = value_in + jnp.einsum(
                "qshk,qshd->kshd",
                attn_prob.astype(jnp.bfloat16),
                grad_part,
                preferred_element_type=jnp.float32,
            )
            return (key_in, value_in)

        query_acc = lax.cond(
            first_row // BLOCK > last_block, lambda acc_in: acc_in, query_update, query_acc
        )
        key_acc, value_acc = lax.cond(
            my_first // BLOCK > (first_row + count - 1) // BLOCK,
            lambda inner: inner,
            key_update,
            (key_acc, value_acc),
        )
        return (query_acc, key_acc, value_acc)

    zero_heads = jnp.zeros(query_heads.shape, jnp.float32)
    query_grad_f, key_grad_f, value_grad_f = by_blocks(
        back_step,
        (zero_heads, zero_heads, zero_heads),
        (
            lax.all_gather(query_three, "ctx", axis=0, tiled=True),
            lax.all_gather(key_three, "ctx", axis=0, tiled=True),
            lax.all_gather(value_three, "ctx", axis=0, tiled=True),
            lax.all_gather(grad_three, "ctx", axis=0, tiled=True),
        ),
    )
    query_grad = query_grad_f.reshape(tokens, head_width).astype(jnp.bfloat16)
    key_grad = key_grad_f.reshape(tokens, head_width).astype(jnp.bfloat16)
    value_grad = value_grad_f.reshape(tokens, head_width).astype(jnp.bfloat16)
    stacked_grad = jnp.stack([query_grad, key_grad, value_grad])
    grad_bias_qv = jnp.stack(
        [
            jnp.sum(query_grad.astype(jnp.float32), axis=0),
            jnp.sum(value_grad.astype(jnp.float32), axis=0),
        ]
    ).reshape(bias_qv.shape)
    grad_qkv = jnp.einsum("td,ctf->cdf", first_in, stacked_grad, preferred_element_type=jnp.float32)
    first_term = jnp.einsum(
        "ctf,cdf->td", stacked_grad, qkv_full, preferred_element_type=jnp.float32
    )
    first_grad = lax.psum(first_term, "tp")
    grad_gain_one = jnp.sum(first_grad * normed_one, axis=0)
    grad_shift_one = jnp.sum(first_grad, axis=0)
    input_rows = own_rows(
        mixed_grad + norm_backward(first_grad, normed_one, spread_one, gain_one_f)
    )
    input_grad = input_rows.astype(jnp.bfloat16).reshape(share_rows, seq_count, model_width)
    shares = (
        lax.psum_scatter(grad_gain_one, ("fsdp", "ctx"), scatter_dimension=0, tiled=True),
        lax.psum_scatter(grad_shift_one, ("fsdp", "ctx"), scatter_dimension=0, tiled=True),
        lax.psum_scatter(grad_qkv, ("fsdp", "ctx"), scatter_dimension=1, tiled=True),
        lax.psum_scatter(grad_bias_qv, ("fsdp", "ctx"), scatter_dimension=2, tiled=True),
        lax.psum_scatter(grad_proj, ("fsdp", "ctx"), scatter_dimension=1, tiled=True),
        lax.psum_scatter(grad_bias_proj, ("fsdp", "ctx"), scatter_dimension=0, tiled=True),
        lax.psum_scatter(grad_gain_two, ("fsdp", "ctx"), scatter_dimension=0, tiled=True),
        lax.psum_scatter(grad_shift_two, ("fsdp", "ctx"), scatter_dimension=0, tiled=True),
        lax.psum_scatter(grad_fc, ("fsdp", "ctx"), scatter_dimension=0, tiled=True),
        lax.psum_scatter(
            grad_bias_fc.reshape(bias_fc.shape), ("fsdp", "ctx"), scatter_dimension=1, tiled=True
        ),
        lax.psum_scatter(grad_fc2, ("fsdp", "ctx"), scatter_dimension=1, tiled=True),
        lax.psum_scatter(grad_bias_fc2, ("fsdp", "ctx"), scatter_dimension=0, tiled=True),
    )
    summed = (
        lax.all_gather(shares[0], "ctx", axis=0, tiled=True),
        lax.all_gather(shares[1], "ctx", axis=0, tiled=True),
        lax.all_gather(shares[2], "ctx", axis=1, tiled=True),
        lax.all_gather(shares[3], "ctx", axis=2, tiled=True),
        lax.all_gather(shares[4], "ctx", axis=1, tiled=True),
        lax.all_gather(shares[5], "ctx", axis=0, tiled=True),
        lax.all_gather(shares[6], "ctx", axis=0, tiled=True),
        lax.all_gather(shares[7], "ctx", axis=0, tiled=True),
        lax.all_gather(shares[8], "ctx", axis=0, tiled=True),
        lax.all_gather(shares[9], "ctx", axis=1, tiled=True),
        lax.all_gather(shares[10], "ctx", axis=1, tiled=True),
        lax.all_gather(shares[11], "ctx", axis=0, tiled=True),
    )
    return (
        output,
        input_grad,
        summed[0],
        summed[1],
        summed[2],
        summed[3],
        summed[4],
        summed[5],
        summed[6],
        summed[7],
        summed[8],
        summed[9],
        summed[10],
        summed[11],
    )


SWAP = ((0, 1), (1, 0))
MATE = ((0, 1), (1, 0), (2, 3), (3, 2))
PEER = ((0, 2), (2, 0), (1, 3), (3, 1))
INWARD = ((0, 1), (3, 2))
MIDDLE = ((1, 2), (2, 1))
OUTWARD = ((1, 0), (2, 3))


def xor_pairs(count, mask):
    return tuple((place, place ^ mask) for place in range(count))


def bf(values):
    return values.astype(jnp.bfloat16)


def f32(values):
    return values.astype(jnp.float32)


def matmul(left, right):
    return jnp.dot(left, right, preferred_element_type=jnp.float32)


def contract(left, right, left_dim, right_dim):
    return lax.dot_general(
        left,
        right,
        (((left_dim,), (right_dim,)), ((), ())),
        preferred_element_type=jnp.float32,
    )


def merged(values):
    return values.reshape(-1, values.shape[-1])


def stack_heads(values):
    heads = values.shape[-1] // HD
    lane_head = lax.broadcasted_iota(jnp.int32, values.shape, 1) // HD
    blank = jnp.zeros_like(values)
    return jnp.concatenate(
        [jnp.where(lane_head == head, values, blank) for head in range(heads)], axis=0
    )


def attend_kernel(query_ref, key_ref, value_ref, out_ref, lse_ref, score_ref, acc_ref):
    block = pl.program_id(0)
    query = merged(query_ref[:, 0])
    rows, width = query.shape
    heads = width // HD
    scale = HD ** (-0.5)

    def score(other, top):
        values = contract(stack_heads(merged(key_ref[:, other])), query, 1, 1)
        values = values.reshape(heads, rows, rows)
        score_ref[other] = values
        return jnp.maximum(top, jnp.max(values, axis=1, keepdims=True))

    top = lax.fori_loop(0, block + 1, score, jnp.full((heads, 1, rows), NEGATIVE, jnp.float32))

    def weigh(other, total):
        values = jnp.exp((score_ref[other] - top) * scale)
        score_ref[other] = values
        return total + jnp.sum(values, axis=1, keepdims=True)

    total = lax.fori_loop(0, block + 1, weigh, jnp.zeros((heads, 1, rows), jnp.float32))
    lse_ref[0] = top * scale + jnp.log(total)
    inverse = 1.0 / total
    acc_ref[...] = jnp.zeros_like(acc_ref)

    def mix(other, unused):
        prob = bf(score_ref[other] * inverse).reshape(heads * rows, rows)
        acc_ref[...] += contract(prob, stack_heads(merged(value_ref[:, other])), 0, 0)
        return unused

    lax.fori_loop(0, block + 1, mix, 0)
    out_ref[:, 0] = bf(acc_ref[...]).reshape(out_ref.shape[0], out_ref.shape[2], width)


def attend_back_kernel(
    query_ref,
    key_ref,
    value_ref,
    out_ref,
    grad_ref,
    lse_ref,
    qkv_grad_ref,
    query_acc,
    key_acc,
    value_acc,
    query_stack,
    grad_stack,
):
    block = pl.program_id(0)
    blocks = pl.num_programs(0)
    query = merged(query_ref[:, 0])
    grad = merged(grad_ref[:, 0])
    rows, width = query.shape
    heads = width // HD
    lane_head = lax.broadcasted_iota(jnp.int32, (rows, width), 1) // HD
    scale = HD ** (-0.5)
    query_stack[...] = stack_heads(query)
    grad_stack[...] = stack_heads(grad)
    products = f32(grad) * f32(merged(out_ref[:, 0]))
    deltas = []
    for head in range(heads):
        column = jnp.sum(jnp.where(lane_head == head, products, 0.0), axis=1, keepdims=True)
        deltas.append(jnp.transpose(jnp.broadcast_to(column, (rows, 128)))[0:1])
    delta = jnp.concatenate(deltas, axis=1)
    lse = jnp.concatenate([lse_ref[0, head] for head in range(heads)], axis=1)
    query_acc[...] = jnp.zeros_like(query_acc)

    @pl.when(block == 0)
    def clear():
        key_acc[...] = jnp.zeros_like(key_acc)
        value_acc[...] = jnp.zeros_like(value_acc)

    def one_block(other, unused):
        key = merged(key_ref[:, other])
        scores = contract(key, query_stack[...], 1, 1)
        prob_grad = contract(merged(value_ref[:, other]), grad_stack[...], 1, 1)
        prob = jnp.exp(scores * scale - lse)
        score_grad = bf(prob * (prob_grad - delta))
        value_acc[other] += contract(bf(prob), grad_stack[...], 1, 0)
        key_acc[other] += contract(score_grad, query_stack[...], 1, 0)
        tall = jnp.concatenate(
            [score_grad[:, head * rows : (head + 1) * rows] for head in range(heads)], axis=0
        )
        query_acc[...] += contract(tall, stack_heads(key), 0, 0)
        return unused

    lax.fori_loop(0, block + 1, one_block, 0)
    slots, _, part, _ = qkv_grad_ref.shape

    def place(which, other, values):
        qkv_grad_ref[:, other, :, which * width : (which + 1) * width] = bf(values).reshape(
            slots, part, width
        )

    place(0, block, query_acc[...] * scale)

    @pl.when(block == blocks - 1)
    def finish():
        for other in range(key_acc.shape[0]):
            place(1, other, key_acc[other] * scale)
            place(2, other, value_acc[other])


def attend_specs(qkv):
    slots, blocks, part, width = qkv.shape
    width //= 3
    one = pl.BlockSpec((slots, 1, part, width), lambda i: (0, i, 0, 0))
    key = pl.BlockSpec((slots, blocks, part, width), lambda i: (0, 0, 0, 1))
    value = pl.BlockSpec((slots, blocks, part, width), lambda i: (0, 0, 0, 2))
    return slots, blocks, part, width, one, key, value


def attend(qkv):
    slots, blocks, part, width, one, key, value = attend_specs(qkv)
    rows = slots * part
    heads = width // HD
    pairs = blocks * (blocks + 1) // 2 * heads
    return pl.pallas_call(
        attend_kernel,
        grid=(blocks,),
        in_specs=[one, key, value],
        out_specs=[one, pl.BlockSpec((1, heads, 1, rows), lambda i: (i, 0, 0, 0))],
        out_shape=[
            jax.ShapeDtypeStruct((slots, blocks, part, width), jnp.bfloat16),
            jax.ShapeDtypeStruct((blocks, heads, 1, rows), jnp.float32),
        ],
        scratch_shapes=[
            pltpu.VMEM((blocks, heads, rows, rows), jnp.float32),
            pltpu.VMEM((rows, width), jnp.float32),
        ],
        cost_estimate=pl.CostEstimate(
            flops=pairs * 4 * rows * rows * width,
            bytes_accessed=8 * qkv.size // 3,
            transcendentals=pairs * rows * rows,
        ),
        name="attend",
    )(qkv, qkv, qkv)


def attend_back(qkv, out, grad, lse):
    slots, blocks, part, width, one, key, value = attend_specs(qkv)
    rows = slots * part
    heads = width // HD
    pairs = blocks * (blocks + 1) // 2 * heads
    return pl.pallas_call(
        attend_back_kernel,
        grid=(blocks,),
        in_specs=[
            one,
            key,
            value,
            one,
            one,
            pl.BlockSpec((1, heads, 1, rows), lambda i: (i, 0, 0, 0)),
        ],
        out_specs=pl.BlockSpec(qkv.shape, lambda i: (0, 0, 0, 0)),
        out_shape=jax.ShapeDtypeStruct(qkv.shape, jnp.bfloat16),
        scratch_shapes=[
            pltpu.VMEM((rows, width), jnp.float32),
            pltpu.VMEM((blocks, rows, width), jnp.float32),
            pltpu.VMEM((blocks, rows, width), jnp.float32),
            pltpu.VMEM((heads * rows, width), jnp.bfloat16),
            pltpu.VMEM((heads * rows, width), jnp.bfloat16),
        ],
        cost_estimate=pl.CostEstimate(
            flops=pairs * 10 * rows * rows * width,
            bytes_accessed=16 * qkv.size // 3,
            transcendentals=pairs * rows * rows,
        ),
        name="attend_back",
    )(qkv, qkv, qkv, out, grad, lse)


def unit_mask(rows, width, start):
    row = lax.broadcasted_iota(jnp.int32, (rows, width), 0)
    unit = lax.broadcasted_iota(jnp.int32, (rows, width), 1) - start
    return jnp.logical_and(unit >= 0, unit // HD == row)


def pick_matrix(width, shift):
    column = lax.broadcasted_iota(jnp.int32, (HD // 2, width), 0)
    unit = lax.broadcasted_iota(jnp.int32, (HD // 2, width), 1)
    return f32(unit % HD == column + shift)


def pack_params_kernel(*refs):
    vectors, qv_ref, fc_ref, out_ref, scratch = refs[:6], *refs[6:]
    scratch[...] = jnp.zeros_like(scratch)
    for row, vector in enumerate(vectors):
        scratch[row, :] = f32(vector[...])
    heads = qv_ref.shape[1]
    part = qv_ref.shape[2]
    for which in range(2):
        scratch[8 + which * heads : 8 + (which + 1) * heads, :part] = f32(qv_ref[which])
        scratch[8:16, 128 * (which + 1) : 128 * (which + 1) + part] = f32(
            fc_ref[8 * which : 8 * which + 8, :]
        )
    out_ref[...] = bf(scratch[...])


def pack_params(vectors, qv_bias, fc_bias):
    shape = (16, vectors[0].shape[0])
    return pl.pallas_call(
        pack_params_kernel,
        out_shape=jax.ShapeDtypeStruct(shape, jnp.bfloat16),
        scratch_shapes=[pltpu.VMEM(shape, jnp.float32)],
        name="pack_params",
    )(*vectors, qv_bias, fc_bias)


def low_high(flag, own, other):
    return jnp.where(flag == 0, own, other), jnp.where(flag == 0, other, own)


def unpack_params_kernel(flag_ref, own_ref, other_ref, vector_ref, qkv_ref, fc_ref):
    flag = flag_ref[0]
    own = f32(own_ref[...])
    other = f32(other_ref[...])
    vector_ref[...] = jnp.concatenate([own[:8], other[:8]], axis=1)
    part = HD // 2

    def spread(width, column):
        low, high = low_high(
            flag, own[8:16, column : column + part], other[8:16, column : column + part]
        )
        return matmul(low, pick_matrix(width, 0)) + matmul(high, pick_matrix(width, part))

    def row_of(values, mask):
        return jnp.sum(jnp.where(mask, values, 0.0), axis=0, keepdims=True)

    width = qkv_ref.shape[1]
    third = width // 3
    heads = third // HD
    row = lax.broadcasted_iota(jnp.int32, (8, width), 0)
    query_mask = jnp.logical_and(unit_mask(8, width, 0), row < heads)
    value_mask = unit_mask(8, width, 2 * third - heads * HD)
    value_mask = jnp.logical_and(value_mask, row >= heads)
    qkv_ref[...] = row_of(spread(width, 0), jnp.logical_or(query_mask, value_mask))
    width = fc_ref.shape[1]
    fc_ref[...] = row_of(spread(width, 128), unit_mask(8, width, 0)) + row_of(
        spread(width, 256), unit_mask(8, width, 8 * HD)
    )


def unpack_params(flag, own, other, qkv_width, fc_width):
    whole = pl.BlockSpec(memory_space=pltpu.VMEM)
    return pl.pallas_call(
        unpack_params_kernel,
        in_specs=[pl.BlockSpec(memory_space=pltpu.SMEM), whole, whole],
        out_shape=[
            jax.ShapeDtypeStruct((8, 2 * own.shape[1]), jnp.float32),
            jax.ShapeDtypeStruct((1, qkv_width), jnp.float32),
            jax.ShapeDtypeStruct((1, fc_width), jnp.float32),
        ],
        name="unpack_params",
    )(flag, own, other)


def pack_sums_kernel(flag_ref, *refs):
    vectors, qkv_ref, fc_ref, kept_ref, sent_ref = refs[:6], *refs[6:]
    flag = flag_ref[0]
    half = kept_ref.shape[1]
    part = HD // 2
    kept_ref[...] = jnp.zeros_like(kept_ref)
    sent_ref[...] = jnp.zeros_like(sent_ref)
    for row, vector in enumerate(vectors):
        kept_ref[row, :] = vector[:half]
        sent_ref[row, :] = vector[half:]

    def take(mask, values, column):
        spread = jnp.where(mask, jnp.broadcast_to(values, mask.shape), 0.0)

        def pick(shift):
            return lax.dot_general(
                spread,
                pick_matrix(mask.shape[1], shift),
                (((1,), (1,)), ((), ())),
                precision=lax.Precision.HIGHEST,
                preferred_element_type=jnp.float32,
            )

        kept, sent = low_high(flag, pick(0), pick(part))
        kept_ref[8:16, column : column + part] = kept
        sent_ref[8:16, column : column + part] = sent

    width = qkv_ref.shape[0]
    third = width // 3
    heads = third // HD
    row = lax.broadcasted_iota(jnp.int32, (8, width), 0)
    query_mask = jnp.logical_and(unit_mask(8, width, 0), row < heads)
    value_mask = jnp.logical_and(unit_mask(8, width, 2 * third - heads * HD), row >= heads)
    take(jnp.logical_or(query_mask, value_mask), qkv_ref[...].reshape(1, width), 0)
    width = fc_ref.shape[0]
    values = fc_ref[...].reshape(1, width)
    take(unit_mask(8, width, 0), values, 128)
    take(unit_mask(8, width, 8 * HD), values, 256)


def pack_sums(flag, vectors, sum_qkv, sum_fc):
    whole = pl.BlockSpec(memory_space=pltpu.VMEM)
    shape = jax.ShapeDtypeStruct((16, vectors[0].shape[0] // 2), jnp.float32)
    return pl.pallas_call(
        pack_sums_kernel,
        in_specs=[pl.BlockSpec(memory_space=pltpu.SMEM)] + [whole] * 8,
        out_shape=[shape, shape],
        name="pack_sums",
    )(flag, *vectors, sum_qkv, sum_fc)


def unpack_sums_kernel(sums_ref, *refs):
    vectors, qv_ref, fc_ref = refs[:6], *refs[6:]
    for row, vector in enumerate(vectors):
        vector[...] = sums_ref[row, :]
    heads, part = qv_ref.shape[1:]
    for which in range(2):
        qv_ref[which] = sums_ref[8 + which * heads : 8 + (which + 1) * heads, :part]
        fc_ref[8 * which : 8 * which + 8, :] = sums_ref[
            8:16, 128 * (which + 1) : 128 * (which + 1) + part
        ]


def unpack_sums(sums, qv_shape, fc_shape):
    vector = jax.ShapeDtypeStruct((sums.shape[1],), jnp.float32)
    return pl.pallas_call(
        unpack_sums_kernel,
        out_shape=[vector] * 6
        + [jax.ShapeDtypeStruct(qv_shape, jnp.float32), jax.ShapeDtypeStruct(fc_shape, jnp.float32)],
        name="unpack_sums",
    )(sums)


def spread_parts(values):
    mate = lax.ppermute(values, "tp", MATE)
    peer = lax.ppermute(values, "tp", PEER)
    across = lax.ppermute(peer, "tp", MATE)
    return (values, mate, peer, across)


def gather_sum(part_of):
    across = lax.ppermute(bf(part_of(3)), "tp", MATE)
    peer = lax.ppermute(bf(part_of(2) + f32(across)), "tp", PEER)
    mate = lax.ppermute(bf(part_of(1)), "tp", MATE)
    return part_of(0) + f32(mate) + f32(peer)


def join_rows(parts):
    return lax.optimization_barrier(jnp.concatenate(parts, axis=0))


def sum_halves(half_of):
    sent = bf(half_of(1))
    other = lax.ppermute(sent, "fsdp", SWAP)
    return bf(half_of(0) + f32(other))


def sum_chained(half_of):
    half = sum_halves(half_of)
    edge = lax.ppermute(half, "ctx", INWARD)
    pair = bf(f32(half) + f32(edge))
    middle = lax.ppermute(pair, "ctx", MIDDLE)
    total = bf(f32(pair) + f32(middle))
    outer = lax.ppermute(total, "ctx", OUTWARD)
    place = lax.axis_index("ctx")
    inner = jnp.logical_and(place > 0, place < 3)
    return f32(jnp.where(inner, total, outer))


def fast_device(
    inputs,
    cotangent,
    ln1_gain,
    ln1_bias,
    qkv_weight,
    qv_bias,
    proj_weight,
    proj_bias,
    ln2_gain,
    ln2_bias,
    fc_weight,
    fc_bias,
    fc2_weight,
    fc2_bias,
):
    row_count, _, width = inputs.shape
    tp_count = lax.axis_size("tp")
    ctx_count = lax.axis_size("ctx")
    share_rows = row_count // tp_count
    share_tokens = share_rows * ctx_count
    place_f = lax.axis_index("fsdp")
    place_c = lax.axis_index("ctx")
    place_t = lax.axis_index("tp")
    half = width // 2
    lower = place_f == 0

    def own_first(values):
        flipped = jnp.concatenate([values[..., half:], values[..., :half]], axis=-1)
        return jnp.where(lower, values, flipped)

    def to_sequences(values):
        mine = lax.dynamic_slice_in_dim(values, place_t * share_rows, share_rows, 0)
        mine = own_first(mine)
        got = []
        for step in range(ctx_count):
            piece = lax.dynamic_index_in_dim(mine, place_c ^ step, 1, keepdims=False)
            if step:
                piece = lax.ppermute(piece, "ctx", xor_pairs(ctx_count, step))
            got.append(piece)
        stacked = jnp.stack(got)
        ordered = [
            lax.dynamic_index_in_dim(stacked, place_c ^ step, 0, keepdims=False)
            for step in range(ctx_count)
        ]
        return jnp.concatenate(ordered, axis=0)

    def to_positions(values):
        mine = own_first(values).reshape(ctx_count, share_rows, width)
        got = []
        for step in range(ctx_count):
            piece = lax.dynamic_index_in_dim(mine, place_c ^ step, 0, keepdims=False)
            if step:
                piece = lax.ppermute(piece, "ctx", xor_pairs(ctx_count, step))
            got.append(piece)
        stacked = jnp.stack(got)
        ordered = [
            lax.dynamic_index_in_dim(stacked, place_c ^ step, 0, keepdims=False)
            for step in range(ctx_count)
        ]
        return jnp.stack(ordered, axis=1)

    flat = f32(to_sequences(inputs))

    flag = place_f.astype(jnp.int32).reshape(1)
    small_own = pack_params(
        (ln1_gain, ln1_bias, proj_bias, ln2_gain, ln2_bias, fc2_bias), qv_bias, fc_bias
    )
    small_other = lax.ppermute(small_own, "fsdp", SWAP)
    qkv_other = lax.ppermute(qkv_weight, "fsdp", SWAP)
    proj_other = lax.ppermute(proj_weight, "fsdp", SWAP)
    fc_other = lax.ppermute(fc_weight, "fsdp", SWAP)
    fc2_other = lax.ppermute(fc2_weight, "fsdp", SWAP)
    proj_full = jnp.concatenate([proj_weight, proj_other], axis=1)
    fc_full = jnp.concatenate([fc_weight, fc_other], axis=0)
    fc2_full = jnp.concatenate([fc2_weight, fc2_other], axis=1)
    qkv_full = jnp.concatenate(
        [
            jnp.concatenate([entry[index] for index in range(3)], axis=1)
            for entry in (qkv_weight, qkv_other)
        ],
        axis=0,
    )

    head_width = qkv_weight.shape[2]
    vectors, bias_qkv, bias_row = unpack_params(
        flag, small_own, small_other, 3 * head_width, fc_weight.shape[1]
    )
    gain_one, shift_one, bias_proj, gain_two, shift_two, bias_fc2 = (vectors[n] for n in range(6))

    first_f, normed_one, spread_one = norm_forward(flat, gain_one, shift_one)
    first_in = join_rows(spread_parts(bf(first_f)))
    head_shape = (tp_count, ctx_count, share_rows, head_width)
    qkv = bf(matmul(first_in, qkv_full) + bias_qkv)
    qkv = qkv.reshape(head_shape[:3] + (3 * head_width,))
    attended_four, lse = attend(qkv)
    attended = attended_four.reshape(-1, head_width)

    def rows_of(values, slot):
        return values[slot * share_tokens : (slot + 1) * share_tokens]

    attn_sum = gather_sum(lambda slot: matmul(rows_of(attended, slot), proj_full))
    mixed = flat + attn_sum + bias_proj
    second_f, normed_two, spread_two = norm_forward(mixed, gain_two, shift_two)
    second_in = spread_parts(bf(second_f))

    grad_own = to_sequences(cotangent)
    grad_rows = spread_parts(grad_own)
    grad_y = f32(grad_own)

    hidden = []
    pre_grad = []
    for slot in range(tp_count):
        hidden_grad = contract(grad_rows[slot], fc2_full, 1, 1)
        pre_act = matmul(second_in[slot], fc_full) + bias_row
        activated, gelu_pull = jax.vjp(partial(jax.nn.gelu, approximate=True), pre_act)
        hidden.append(bf(activated))
        pre_grad.append(bf(gelu_pull(hidden_grad)[0]))

    second_grad = gather_sum(lambda slot: contract(pre_grad[slot], fc_full, 1, 1))
    mixed_grad = grad_y + norm_backward(second_grad, normed_two, spread_two, gain_two)
    branch_own = bf(mixed_grad)
    branch = spread_parts(branch_own)

    mlp_sum = gather_sum(lambda slot: matmul(hidden[slot], fc2_full))
    output = to_positions(bf(mixed + mlp_sum + bias_fc2))

    def halved(values, which):
        return values[:, which * half : (which + 1) * half]

    hidden_all = join_rows(hidden)
    pre_grad_all = join_rows(pre_grad)
    second_all = join_rows(second_in)
    grad_all = join_rows(grad_rows)
    grad_fc2 = sum_chained(lambda which: contract(hidden_all, halved(grad_all, which), 0, 0))
    grad_fc = sum_chained(lambda which: contract(halved(second_all, which), pre_grad_all, 0, 0))

    branch = join_rows(branch)
    attended_grad = bf(contract(branch, proj_full, 1, 1)).reshape(head_shape)
    qkv_grad = attend_back(qkv, attended_four, attended_grad, lse).reshape(-1, 3 * head_width)
    grad_proj = sum_chained(lambda which: contract(attended, halved(branch, which), 0, 0))
    grad_qkv = sum_chained(lambda which: contract(halved(first_in, which), qkv_grad, 0, 0))
    grad_qkv = jnp.stack(
        [grad_qkv[:, index * head_width : (index + 1) * head_width] for index in range(3)]
    )

    first_grad = gather_sum(lambda slot: contract(rows_of(qkv_grad, slot), qkv_full, 1, 1))
    input_own = mixed_grad + norm_backward(first_grad, normed_one, spread_one, gain_one)
    input_grad = to_positions(bf(input_own))

    token_sums = (
        jnp.sum(first_grad * normed_one, axis=0),
        jnp.sum(first_grad, axis=0),
        jnp.sum(f32(branch_own), axis=0),
        jnp.sum(second_grad * normed_two, axis=0),
        jnp.sum(second_grad, axis=0),
        jnp.sum(grad_y, axis=0),
    )
    sum_qkv = jnp.sum(f32(qkv_grad), axis=0)
    sum_fc = sum(jnp.sum(f32(part), axis=0) for part in pre_grad)
    kept, sent = pack_sums(flag, token_sums, sum_qkv, sum_fc)
    small = kept + lax.ppermute(sent, "fsdp", SWAP)
    shared = small[:8]
    shared = shared + lax.ppermute(shared, "tp", MATE)
    shared = shared + lax.ppermute(shared, "tp", PEER)
    small = jnp.concatenate([shared, small[8:]], axis=0)
    small = small + lax.ppermute(small, "ctx", xor_pairs(ctx_count, 1))
    small = small + lax.ppermute(small, "ctx", xor_pairs(ctx_count, 2))
    sums = unpack_sums(small, qv_bias.shape, fc_bias.shape)
    return (
        output,
        input_grad,
        sums[0],
        sums[1],
        grad_qkv,
        sums[6],
        grad_proj,
        sums[2],
        sums[3],
        sums[4],
        grad_fc,
        sums[7],
        grad_fc2,
        sums[5],
    )


def on_device(*args):
    rows, sequences, _ = args[0].shape
    whole_sequences = (
        lax.axis_size("fsdp") == 2
        and lax.axis_size("tp") == 4
        and lax.axis_size("ctx") == 4
        and sequences == 4
        and rows == BLOCK
    )
    if not whole_sequences:
        return general_device(*args)
    return fast_device(*args)


def solution(mesh):
    return jax.shard_map(
        on_device,
        mesh=mesh,
        in_specs=(
            P("ctx", "fsdp", None),
            P("ctx", "fsdp", None),
            P("fsdp"),
            P("fsdp"),
            P(None, "fsdp", "tp"),
            P(None, "tp", "fsdp"),
            P("tp", "fsdp"),
            P("fsdp"),
            P("fsdp"),
            P("fsdp"),
            P("fsdp", "tp"),
            P("tp", "fsdp"),
            P("tp", "fsdp"),
            P("fsdp"),
        ),
        out_specs=(
            P(("ctx", "tp"), "fsdp", None),
            P(("ctx", "tp"), "fsdp", None),
            P("fsdp"),
            P("fsdp"),
            P(None, "fsdp", "tp"),
            P(None, "tp", "fsdp"),
            P("tp", "fsdp"),
            P("fsdp"),
            P("fsdp"),
            P("fsdp"),
            P("fsdp", "tp"),
            P("tp", "fsdp"),
            P("tp", "fsdp"),
            P("fsdp"),
        ),
        check_vma=False,
    )
```

```python
from functools import partial
import math

import jax
import jax.numpy as jnp
from jax import lax
from jax.experimental import pallas as pl
from jax.experimental.pallas import tpu as pltpu
from jax.sharding import PartitionSpec as P


HD = 64
BLOCK = 256


EPSILON = 1e-05
NEGATIVE = -1e30
SUB_ROWS = 512


def norm_forward(values, gain, shift):
    centred = values - jnp.mean(values, axis=-1, keepdims=True)
    spread = lax.rsqrt(jnp.mean(centred * centred, axis=-1, keepdims=True) + EPSILON)
    normed = centred * spread
    return (normed * gain + shift, normed, spread)


def norm_backward(grad_out, normed, spread, gain):
    scaled = grad_out * gain
    return spread * (
        scaled
        - jnp.mean(scaled, axis=-1, keepdims=True)
        - normed * jnp.mean(scaled * normed, axis=-1, keepdims=True)
    )


def left_inner(left, right):
    return lax.dot_general(
        left, right, (((0,), (0,)), ((), ())), preferred_element_type=jnp.float32
    )


def right_inner(left, right):
    return lax.dot_general(
        left, right, (((1,), (1,)), ((), ())), preferred_element_type=jnp.float32
    )


def split_heads(values):
    return values.reshape(values.shape[0], values.shape[1], -1, HD)


def block_scores(query_heads, key_heads, query_pos, key_pos):
    scores = jnp.einsum(
        "qshd,kshd->qshk", query_heads, key_heads, preferred_element_type=jnp.float32
    ) * HD ** (-0.5)
    allowed = key_pos[None, :] // BLOCK <= query_pos[:, None] // BLOCK
    return (scores, allowed[:, None, None, :])


def by_blocks(step_fn, carry, pieces):
    count = pieces[0].shape[0]
    sub_width = math.gcd(count, SUB_ROWS)
    split = tuple(
        (entry.reshape((count // sub_width, sub_width) + entry.shape[1:]) for entry in pieces)
    )

    def advance(state, item):
        block_index, parts = item
        return (step_fn(state, parts, block_index * sub_width), None)

    state, _ = lax.scan(advance, carry, (jnp.arange(count // sub_width, dtype=jnp.int32), split))
    return state


def general_device(
    inputs,
    cotangent,
    ln1_gain,
    ln1_bias,
    qkv_weight,
    qv_bias,
    proj_weight,
    proj_bias,
    ln2_gain,
    ln2_bias,
    fc_weight,
    fc_bias,
    fc2_weight,
    fc2_bias,
):
    row_count, seq_count, model_width = inputs.shape
    tokens = row_count * seq_count
    tp_count = lax.axis_size("tp")
    share_rows = row_count // tp_count
    share_tokens = share_rows * seq_count
    share_first = lax.axis_index("tp") * share_tokens

    def own_rows(values):
        return lax.dynamic_slice_in_dim(values, share_first, share_tokens, 0)

    gathered = (
        lax.all_gather(ln1_gain, "fsdp", axis=0, tiled=True),
        lax.all_gather(ln1_bias, "fsdp", axis=0, tiled=True),
        lax.all_gather(qkv_weight, "fsdp", axis=1, tiled=True),
        lax.all_gather(qv_bias, "fsdp", axis=2, tiled=True),
        lax.all_gather(proj_weight, "fsdp", axis=1, tiled=True),
        lax.all_gather(proj_bias, "fsdp", axis=0, tiled=True),
        lax.all_gather(ln2_gain, "fsdp", axis=0, tiled=True),
        lax.all_gather(ln2_bias, "fsdp", axis=0, tiled=True),
        lax.all_gather(fc_weight, "fsdp", axis=0, tiled=True),
        lax.all_gather(fc_bias, "fsdp", axis=1, tiled=True),
        lax.all_gather(fc2_weight, "fsdp", axis=1, tiled=True),
        lax.all_gather(fc2_bias, "fsdp", axis=0, tiled=True),
    )
    (
        gain_one,
        shift_one,
        qkv_full,
        bias_qv,
        proj_full,
        bias_proj,
        gain_two,
        shift_two,
        fc_full,
        bias_fc,
        fc2_full,
        bias_fc2,
    ) = gathered
    head_width = qkv_full.shape[2]
    gain_one_f = gain_one.astype(jnp.float32)
    gain_two_f = gain_two.astype(jnp.float32)
    flat = inputs.reshape(tokens, model_width).astype(jnp.float32)
    first_f, normed_one, spread_one = norm_forward(flat, gain_one_f, shift_one.astype(jnp.float32))
    first_in = first_f.astype(jnp.bfloat16)
    bias_rows = bias_qv.reshape(2, head_width).astype(jnp.float32)
    projected = jnp.einsum("td,cdf->ctf", first_in, qkv_full, preferred_element_type=jnp.float32)
    query_three = (
        (projected[0] + bias_rows[0]).astype(jnp.bfloat16).reshape(row_count, seq_count, head_width)
    )
    key_three = projected[1].astype(jnp.bfloat16).reshape(row_count, seq_count, head_width)
    value_three = (
        (projected[2] + bias_rows[1]).astype(jnp.bfloat16).reshape(row_count, seq_count, head_width)
    )
    query_heads = split_heads(query_three)
    key_heads = split_heads(key_three)
    value_heads = split_heads(value_three)
    local_heads = query_heads.shape[2]
    cycle_place = lax.axis_index("ctx")
    my_first = cycle_place * row_count
    my_pos = my_first + jnp.arange(row_count, dtype=jnp.int32)
    last_block = (my_first + row_count - 1) // BLOCK
    scale = HD ** (-0.5)

    def forward_step(state, parts, first_row):
        key_part, value_part = parts
        key_pos = first_row + jnp.arange(key_part.shape[0], dtype=jnp.int32)

        def update(inner):
            acc_sum, row_top, denom_sum = inner
            scores, allowed = block_scores(query_heads, split_heads(key_part), my_pos, key_pos)
            scores = jnp.where(allowed, scores, NEGATIVE)
            new_top = jnp.maximum(row_top, jnp.max(scores, axis=-1))
            rescale = jnp.exp(row_top - new_top)
            block_weights = jnp.where(allowed, jnp.exp(scores - new_top[..., None]), 0.0)
            denom_sum = denom_sum * rescale + jnp.sum(block_weights, axis=-1)
            acc_sum = acc_sum * rescale[..., None] + jnp.einsum(
                "qshk,kshd->qshd",
                block_weights.astype(jnp.bfloat16),
                split_heads(value_part),
                preferred_element_type=jnp.float32,
            )
            return (acc_sum, new_top, denom_sum)

        return lax.cond(first_row // BLOCK > last_block, lambda inner: inner, update, state)

    stat_shape = (row_count, seq_count, local_heads)
    start_state = (
        jnp.zeros(query_heads.shape, jnp.float32),
        jnp.full(stat_shape, NEGATIVE, jnp.float32),
        jnp.zeros(stat_shape, jnp.float32),
    )
    acc_sum, row_top, denom_sum = by_blocks(
        forward_step,
        start_state,
        (
            lax.all_gather(key_three, "ctx", axis=0, tiled=True),
            lax.all_gather(value_three, "ctx", axis=0, tiled=True),
        ),
    )
    attended_f = acc_sum / denom_sum[..., None]
    log_total = row_top + jnp.log(denom_sum)
    attended = attended_f.reshape(tokens, head_width).astype(jnp.bfloat16)
    attn_term = jnp.dot(attended, proj_full, preferred_element_type=jnp.float32)
    mixed_rows = flat + lax.psum(attn_term, "tp") + bias_proj.astype(jnp.float32)
    second_f, normed_two, spread_two = norm_forward(
        mixed_rows, gain_two_f, shift_two.astype(jnp.float32)
    )
    second_in = second_f.astype(jnp.bfloat16)
    pre_act = jnp.dot(second_in, fc_full, preferred_element_type=jnp.float32) + bias_fc.reshape(
        -1
    ).astype(jnp.float32)
    activated, gelu_pull = jax.vjp(partial(jax.nn.gelu, approximate=True), pre_act)
    hidden = activated.astype(jnp.bfloat16)
    mlp_term = jnp.dot(hidden, fc2_full, preferred_element_type=jnp.float32)
    final_share = own_rows(mixed_rows + lax.psum(mlp_term, "tp") + bias_fc2.astype(jnp.float32))
    output = final_share.astype(jnp.bfloat16).reshape(share_rows, seq_count, model_width)
    grad_rows = cotangent.reshape(tokens, model_width)
    grad_y = grad_rows.astype(jnp.float32)
    grad_bias_fc2 = jnp.sum(grad_y, axis=0)
    grad_fc2 = left_inner(hidden, grad_rows)
    hidden_grad = right_inner(grad_rows, fc2_full)
    (pre_grad_f,) = gelu_pull(hidden_grad)
    pre_grad = pre_grad_f.astype(jnp.bfloat16)
    grad_bias_fc = jnp.sum(pre_grad.astype(jnp.float32), axis=0)
    grad_fc = left_inner(second_in, pre_grad)
    second_term = right_inner(pre_grad, fc_full)
    second_grad = lax.psum(second_term, "tp")
    grad_gain_two = jnp.sum(second_grad * normed_two, axis=0)
    grad_shift_two = jnp.sum(second_grad, axis=0)
    mixed_grad = grad_y + norm_backward(second_grad, normed_two, spread_two, gain_two_f)
    branch_grad = mixed_grad.astype(jnp.bfloat16)
    grad_bias_proj = jnp.sum(branch_grad.astype(jnp.float32), axis=0)
    grad_proj = left_inner(attended, branch_grad)
    attended_grad = right_inner(branch_grad, proj_full).astype(jnp.bfloat16)
    grad_three = attended_grad.reshape(row_count, seq_count, head_width)
    grad_heads = split_heads(grad_three)
    delta_rows = jnp.sum(grad_heads.astype(jnp.float32) * attended_f, axis=-1)
    lse_all, delta_all = (
        lax.all_gather(log_total, "ctx", axis=0, tiled=True),
        lax.all_gather(delta_rows, "ctx", axis=0, tiled=True),
    )

    def back_step(state, parts, first_row):
        query_part_flat, key_part_flat, value_part_flat, grad_part_flat = parts
        count = query_part_flat.shape[0]
        other_pos = first_row + jnp.arange(count, dtype=jnp.int32)
        query_acc, key_acc, value_acc = state

        def query_update(acc_in):
            key_part = split_heads(key_part_flat)
            scores, allowed = block_scores(query_heads, key_part, my_pos, other_pos)
            attn_prob = jnp.where(allowed, jnp.exp(scores - log_total[..., None]), 0.0)
            prob_grad = jnp.einsum(
                "qshd,kshd->qshk",
                grad_heads,
                split_heads(value_part_flat),
                preferred_element_type=jnp.float32,
            )
            score_grad = (attn_prob * (prob_grad - delta_rows[..., None])).astype(jnp.bfloat16)
            return (
                acc_in
                + jnp.einsum(
                    "qshk,kshd->qshd", score_grad, key_part, preferred_element_type=jnp.float32
                )
                * scale
            )

        def key_update(inner):
            key_in, value_in = inner
            lse_part = lax.dynamic_slice_in_dim(lse_all, first_row, count, 0)
            delta_part = lax.dynamic_slice_in_dim(delta_all, first_row, count, 0)
            query_part = split_heads(query_part_flat)
            grad_part = split_heads(grad_part_flat)
            scores, allowed = block_scores(query_part, key_heads, other_pos, my_pos)
            attn_prob = jnp.where(allowed, jnp.exp(scores - lse_part[..., None]), 0.0)
            prob_grad = jnp.einsum(
                "qshd,kshd->qshk", grad_part, value_heads, preferred_element_type=jnp.float32
            )
            score_grad = (attn_prob * (prob_grad - delta_part[..., None])).astype(jnp.bfloat16)
            key_in = (
                key_in
                + jnp.einsum(
                    "qshk,qshd->kshd", score_grad, query_part, preferred_element_type=jnp.float32
                )
                * scale
            )
            value_in = value_in + jnp.einsum(
                "qshk,qshd->kshd",
                attn_prob.astype(jnp.bfloat16),
                grad_part,
                preferred_element_type=jnp.float32,
            )
            return (key_in, value_in)

        query_acc = lax.cond(
            first_row // BLOCK > last_block, lambda acc_in: acc_in, query_update, query_acc
        )
        key_acc, value_acc = lax.cond(
            my_first // BLOCK > (first_row + count - 1) // BLOCK,
            lambda inner: inner,
            key_update,
            (key_acc, value_acc),
        )
        return (query_acc, key_acc, value_acc)

    zero_heads = jnp.zeros(query_heads.shape, jnp.float32)
    query_grad_f, key_grad_f, value_grad_f = by_blocks(
        back_step,
        (zero_heads, zero_heads, zero_heads),
        (
            lax.all_gather(query_three, "ctx", axis=0, tiled=True),
            lax.all_gather(key_three, "ctx", axis=0, tiled=True),
            lax.all_gather(value_three, "ctx", axis=0, tiled=True),
            lax.all_gather(grad_three, "ctx", axis=0, tiled=True),
        ),
    )
    query_grad = query_grad_f.reshape(tokens, head_width).astype(jnp.bfloat16)
    key_grad = key_grad_f.reshape(tokens, head_width).astype(jnp.bfloat16)
    value_grad = value_grad_f.reshape(tokens, head_width).astype(jnp.bfloat16)
    stacked_grad = jnp.stack([query_grad, key_grad, value_grad])
    grad_bias_qv = jnp.stack(
        [
            jnp.sum(query_grad.astype(jnp.float32), axis=0),
            jnp.sum(value_grad.astype(jnp.float32), axis=0),
        ]
    ).reshape(bias_qv.shape)
    grad_qkv = jnp.einsum("td,ctf->cdf", first_in, stacked_grad, preferred_element_type=jnp.float32)
    first_term = jnp.einsum(
        "ctf,cdf->td", stacked_grad, qkv_full, preferred_element_type=jnp.float32
    )
    first_grad = lax.psum(first_term, "tp")
    grad_gain_one = jnp.sum(first_grad * normed_one, axis=0)
    grad_shift_one = jnp.sum(first_grad, axis=0)
    input_rows = own_rows(
        mixed_grad + norm_backward(first_grad, normed_one, spread_one, gain_one_f)
    )
    input_grad = input_rows.astype(jnp.bfloat16).reshape(share_rows, seq_count, model_width)
    shares = (
        lax.psum_scatter(grad_gain_one, ("fsdp", "ctx"), scatter_dimension=0, tiled=True),
        lax.psum_scatter(grad_shift_one, ("fsdp", "ctx"), scatter_dimension=0, tiled=True),
        lax.psum_scatter(grad_qkv, ("fsdp", "ctx"), scatter_dimension=1, tiled=True),
        lax.psum_scatter(grad_bias_qv, ("fsdp", "ctx"), scatter_dimension=2, tiled=True),
        lax.psum_scatter(grad_proj, ("fsdp", "ctx"), scatter_dimension=1, tiled=True),
        lax.psum_scatter(grad_bias_proj, ("fsdp", "ctx"), scatter_dimension=0, tiled=True),
        lax.psum_scatter(grad_gain_two, ("fsdp", "ctx"), scatter_dimension=0, tiled=True),
        lax.psum_scatter(grad_shift_two, ("fsdp", "ctx"), scatter_dimension=0, tiled=True),
        lax.psum_scatter(grad_fc, ("fsdp", "ctx"), scatter_dimension=0, tiled=True),
        lax.psum_scatter(
            grad_bias_fc.reshape(bias_fc.shape), ("fsdp", "ctx"), scatter_dimension=1, tiled=True
        ),
        lax.psum_scatter(grad_fc2, ("fsdp", "ctx"), scatter_dimension=1, tiled=True),
        lax.psum_scatter(grad_bias_fc2, ("fsdp", "ctx"), scatter_dimension=0, tiled=True),
    )
    summed = (
        lax.all_gather(shares[0], "ctx", axis=0, tiled=True),
        lax.all_gather(shares[1], "ctx", axis=0, tiled=True),
        lax.all_gather(shares[2], "ctx", axis=1, tiled=True),
        lax.all_gather(shares[3], "ctx", axis=2, tiled=True),
        lax.all_gather(shares[4], "ctx", axis=1, tiled=True),
        lax.all_gather(shares[5], "ctx", axis=0, tiled=True),
        lax.all_gather(shares[6], "ctx", axis=0, tiled=True),
        lax.all_gather(shares[7], "ctx", axis=0, tiled=True),
        lax.all_gather(shares[8], "ctx", axis=0, tiled=True),
        lax.all_gather(shares[9], "ctx", axis=1, tiled=True),
        lax.all_gather(shares[10], "ctx", axis=1, tiled=True),
        lax.all_gather(shares[11], "ctx", axis=0, tiled=True),
    )
    return (
        output,
        input_grad,
        summed[0],
        summed[1],
        summed[2],
        summed[3],
        summed[4],
        summed[5],
        summed[6],
        summed[7],
        summed[8],
        summed[9],
        summed[10],
        summed[11],
    )


SWAP = ((0, 1), (1, 0))
MATE = ((0, 1), (1, 0), (2, 3), (3, 2))
PEER = ((0, 2), (2, 0), (1, 3), (3, 1))
INWARD = ((0, 1), (3, 2))
MIDDLE = ((1, 2), (2, 1))
OUTWARD = ((1, 0), (2, 3))


def xor_pairs(count, mask):
    return tuple((place, place ^ mask) for place in range(count))


def bf(values):
    return values.astype(jnp.bfloat16)


def f32(values):
    return values.astype(jnp.float32)


def matmul(left, right):
    return jnp.dot(left, right, preferred_element_type=jnp.float32)


def contract(left, right, left_dim, right_dim):
    return lax.dot_general(
        left,
        right,
        (((left_dim,), (right_dim,)), ((), ())),
        preferred_element_type=jnp.float32,
    )


def merged(values):
    return values.reshape(-1, values.shape[-1])


def stack_heads(values):
    heads = values.shape[-1] // HD
    lane_head = lax.broadcasted_iota(jnp.int32, values.shape, 1) // HD
    blank = jnp.zeros_like(values)
    return jnp.concatenate(
        [jnp.where(lane_head == head, values, blank) for head in range(heads)], axis=0
    )


def attend_kernel(place_ref, query_ref, key_ref, value_ref, out_ref, lse_ref, score_ref, acc_ref):
    block = pl.program_id(0)
    place = place_ref[0]
    query = merged(query_ref[:, 0])
    rows, width = query.shape
    heads = width // HD
    scale = HD ** (-0.5)

    def score(other, top):
        values = contract(stack_heads(merged(key_ref[:, other ^ place])), query, 1, 1)
        values = values.reshape(heads, rows, rows)
        score_ref[other] = values
        return jnp.maximum(top, jnp.max(values, axis=1, keepdims=True))

    top = lax.fori_loop(0, block + 1, score, jnp.full((heads, 1, rows), NEGATIVE, jnp.float32))

    acc_ref[...] = jnp.zeros_like(acc_ref)

    def weigh(other, total):
        values = jnp.exp((score_ref[other] - top) * scale)
        prob = bf(values).reshape(heads * rows, rows)
        acc_ref[...] += contract(prob, stack_heads(merged(value_ref[:, other ^ place])), 0, 0)
        return total + jnp.sum(values, axis=1, keepdims=True)

    total = lax.fori_loop(0, block + 1, weigh, jnp.zeros((heads, 1, rows), jnp.float32))
    lse_ref[0] = top * scale + jnp.log(total)
    inverse = 1.0 / total
    lane = lax.broadcasted_iota(jnp.int32, (rows, 2 * HD), 1)
    columns = [
        jnp.transpose(jnp.broadcast_to(inverse[head], (2 * HD, rows))) for head in range(heads)
    ]
    factor = jnp.concatenate(
        [
            jnp.where(lane < HD, columns[head], columns[head + 1])
            for head in range(0, heads, 2)
        ],
        axis=1,
    )
    out_ref[:, 0] = bf(acc_ref[...] * factor).reshape(out_ref.shape[0], out_ref.shape[2], width)


def attend_back_kernel(
    place_ref,
    query_ref,
    key_ref,
    value_ref,
    out_ref,
    grad_ref,
    lse_ref,
    qkv_grad_ref,
    query_acc,
    key_acc,
    value_acc,
    query_stack,
    grad_stack,
):
    block = pl.program_id(0)
    place = place_ref[0]
    blocks = pl.num_programs(0)
    query = merged(query_ref[:, 0])
    grad = merged(grad_ref[:, 0])
    rows, width = query.shape
    heads = width // HD
    lane_head = lax.broadcasted_iota(jnp.int32, (rows, width), 1) // HD
    scale = HD ** (-0.5)
    query_stack[...] = stack_heads(query)
    grad_stack[...] = stack_heads(grad)
    products = f32(grad) * f32(merged(out_ref[:, 0]))
    deltas = []
    for head in range(heads):
        column = jnp.sum(jnp.where(lane_head == head, products, 0.0), axis=1, keepdims=True)
        deltas.append(jnp.transpose(jnp.broadcast_to(column, (rows, 128)))[0:1])
    delta = jnp.concatenate(deltas, axis=1)
    lse = jnp.concatenate([lse_ref[0, head] for head in range(heads)], axis=1)
    query_acc[...] = jnp.zeros_like(query_acc)

    @pl.when(block == 0)
    def clear():
        key_acc[...] = jnp.zeros_like(key_acc)
        value_acc[...] = jnp.zeros_like(value_acc)

    def one_block(other, unused):
        key = merged(key_ref[:, other ^ place])
        scores = contract(key, query_stack[...], 1, 1)
        prob_grad = contract(merged(value_ref[:, other ^ place]), grad_stack[...], 1, 1)
        prob = jnp.exp(scores * scale - lse)
        score_grad = bf(prob * (prob_grad - delta))
        value_acc[other] += contract(bf(prob), grad_stack[...], 1, 0)
        key_acc[other] += contract(score_grad, query_stack[...], 1, 0)
        tall = jnp.concatenate(
            [score_grad[:, head * rows : (head + 1) * rows] for head in range(heads)], axis=0
        )
        query_acc[...] += contract(tall, stack_heads(key), 0, 0)
        return unused

    lax.fori_loop(0, block + 1, one_block, 0)
    slots, _, part, _ = qkv_grad_ref.shape

    def store(which, other, values):
        qkv_grad_ref[:, other ^ place, :, which * width : (which + 1) * width] = bf(values).reshape(
            slots, part, width
        )

    store(0, block, query_acc[...] * scale)

    @pl.when(block == blocks - 1)
    def finish():
        for other in range(key_acc.shape[0]):
            store(1, other, key_acc[other] * scale)
            store(2, other, value_acc[other])


def attend_specs(qkv):
    slots, blocks, part, width = qkv.shape
    width //= 3
    one = pl.BlockSpec((slots, 1, part, width), lambda i, place: (0, i ^ place[0], 0, 0))
    key = pl.BlockSpec((slots, blocks, part, width), lambda i, place: (0, 0, 0, 1))
    value = pl.BlockSpec((slots, blocks, part, width), lambda i, place: (0, 0, 0, 2))
    return slots, blocks, part, width, one, key, value


def attend(place, qkv):
    slots, blocks, part, width, one, key, value = attend_specs(qkv)
    rows = slots * part
    heads = width // HD
    pairs = blocks * (blocks + 1) // 2 * heads
    return pl.pallas_call(
        attend_kernel,
        grid_spec=pltpu.PrefetchScalarGridSpec(
            num_scalar_prefetch=1,
            grid=(blocks,),
            in_specs=[one, key, value],
            out_specs=[one, pl.BlockSpec((1, heads, 1, rows), lambda i, place: (i, 0, 0, 0))],
            scratch_shapes=[
            pltpu.VMEM((blocks, heads, rows, rows), jnp.float32),
            pltpu.VMEM((rows, width), jnp.float32),
        ],
        ),
        out_shape=[
            jax.ShapeDtypeStruct((slots, blocks, part, width), jnp.bfloat16),
            jax.ShapeDtypeStruct((blocks, heads, 1, rows), jnp.float32),
        ],
        cost_estimate=pl.CostEstimate(
            flops=pairs * 4 * rows * rows * width,
            bytes_accessed=8 * qkv.size // 3,
            transcendentals=pairs * rows * rows,
        ),
        name="attend",
    )(place, qkv, qkv, qkv)


def attend_back(place, qkv, out, grad, lse):
    slots, blocks, part, width, one, key, value = attend_specs(qkv)
    rows = slots * part
    heads = width // HD
    pairs = blocks * (blocks + 1) // 2 * heads
    return pl.pallas_call(
        attend_back_kernel,
        grid_spec=pltpu.PrefetchScalarGridSpec(
            num_scalar_prefetch=1,
            grid=(blocks,),
            in_specs=[
            one,
            key,
            value,
            one,
            one,
            pl.BlockSpec((1, heads, 1, rows), lambda i, place: (i, 0, 0, 0)),
        ],
            out_specs=pl.BlockSpec(qkv.shape, lambda i, place: (0, 0, 0, 0)),
            scratch_shapes=[
            pltpu.VMEM((rows, width), jnp.float32),
            pltpu.VMEM((blocks, rows, width), jnp.float32),
            pltpu.VMEM((blocks, rows, width), jnp.float32),
            pltpu.VMEM((heads * rows, width), jnp.bfloat16),
            pltpu.VMEM((heads * rows, width), jnp.bfloat16),
        ],
        ),
        out_shape=jax.ShapeDtypeStruct(qkv.shape, jnp.bfloat16),
        cost_estimate=pl.CostEstimate(
            flops=pairs * 10 * rows * rows * width,
            bytes_accessed=16 * qkv.size // 3,
            transcendentals=pairs * rows * rows,
        ),
        name="attend_back",
    )(place, qkv, qkv, qkv, out, grad, lse)


def unit_mask(rows, width, start):
    row = lax.broadcasted_iota(jnp.int32, (rows, width), 0)
    unit = lax.broadcasted_iota(jnp.int32, (rows, width), 1) - start
    return jnp.logical_and(unit >= 0, unit // HD == row)


def pick_matrix(width, shift):
    column = lax.broadcasted_iota(jnp.int32, (HD // 2, width), 0)
    unit = lax.broadcasted_iota(jnp.int32, (HD // 2, width), 1)
    return f32(unit % HD == column + shift)


def pack_params_kernel(*refs):
    vectors, qv_ref, fc_ref, out_ref, scratch = refs[:6], *refs[6:]
    scratch[...] = jnp.zeros_like(scratch)
    for row, vector in enumerate(vectors):
        scratch[row, :] = f32(vector[...])
    heads = qv_ref.shape[1]
    part = qv_ref.shape[2]
    for which in range(2):
        scratch[8 + which * heads : 8 + (which + 1) * heads, :part] = f32(qv_ref[which])
        scratch[8:16, 128 * (which + 1) : 128 * (which + 1) + part] = f32(
            fc_ref[8 * which : 8 * which + 8, :]
        )
    out_ref[...] = bf(scratch[...])


def pack_params(vectors, qv_bias, fc_bias):
    shape = (16, vectors[0].shape[0])
    return pl.pallas_call(
        pack_params_kernel,
        out_shape=jax.ShapeDtypeStruct(shape, jnp.bfloat16),
        scratch_shapes=[pltpu.VMEM(shape, jnp.float32)],
        name="pack_params",
    )(*vectors, qv_bias, fc_bias)


def low_high(flag, own, other):
    return jnp.where(flag == 0, own, other), jnp.where(flag == 0, other, own)


def unpack_params_kernel(flag_ref, own_ref, other_ref, *refs):
    vectors, qkv_ref, fc_ref = refs[:6], *refs[6:]
    flag = flag_ref[0]
    own = f32(own_ref[...])
    other = f32(other_ref[...])
    for row, vector in enumerate(vectors):
        vector[...] = jnp.concatenate([own[row : row + 1], other[row : row + 1]], axis=1)
    part = HD // 2

    def spread(width, column):
        low, high = low_high(
            flag, own[8:16, column : column + part], other[8:16, column : column + part]
        )
        return matmul(low, pick_matrix(width, 0)) + matmul(high, pick_matrix(width, part))

    def row_of(values, mask):
        return jnp.sum(jnp.where(mask, values, 0.0), axis=0, keepdims=True)

    width = qkv_ref.shape[1]
    third = width // 3
    heads = third // HD
    row = lax.broadcasted_iota(jnp.int32, (8, width), 0)
    query_mask = jnp.logical_and(unit_mask(8, width, 0), row < heads)
    value_mask = unit_mask(8, width, 2 * third - heads * HD)
    value_mask = jnp.logical_and(value_mask, row >= heads)
    qkv_ref[...] = row_of(spread(width, 0), jnp.logical_or(query_mask, value_mask))
    width = fc_ref.shape[1]
    fc_ref[...] = row_of(spread(width, 128), unit_mask(8, width, 0)) + row_of(
        spread(width, 256), unit_mask(8, width, 8 * HD)
    )


def unpack_params(flag, own, other, qkv_width, fc_width):
    whole = pl.BlockSpec(memory_space=pltpu.VMEM)
    return pl.pallas_call(
        unpack_params_kernel,
        in_specs=[pl.BlockSpec(memory_space=pltpu.SMEM), whole, whole],
        out_shape=[jax.ShapeDtypeStruct((1, 2 * own.shape[1]), jnp.float32)] * 6
        + [
            jax.ShapeDtypeStruct((1, qkv_width), jnp.float32),
            jax.ShapeDtypeStruct((1, fc_width), jnp.float32),
        ],
        name="unpack_params",
    )(flag, own, other)


def pack_sums_kernel(flag_ref, *refs):
    vectors, qkv_ref, fc_ref, kept_ref, sent_ref = refs[:6], *refs[6:]
    flag = flag_ref[0]
    half = kept_ref.shape[1]
    part = HD // 2
    kept_ref[...] = jnp.zeros_like(kept_ref)
    sent_ref[...] = jnp.zeros_like(sent_ref)
    for row, vector in enumerate(vectors):
        kept_ref[row, :] = vector[:half]
        sent_ref[row, :] = vector[half:]

    def take(mask, values, column):
        spread = jnp.where(mask, jnp.broadcast_to(values, mask.shape), 0.0)

        def pick(shift):
            return lax.dot_general(
                spread,
                pick_matrix(mask.shape[1], shift),
                (((1,), (1,)), ((), ())),
                precision=lax.Precision.HIGHEST,
                preferred_element_type=jnp.float32,
            )

        kept, sent = low_high(flag, pick(0), pick(part))
        kept_ref[8:16, column : column + part] = kept
        sent_ref[8:16, column : column + part] = sent

    width = qkv_ref.shape[0]
    third = width // 3
    heads = third // HD
    row = lax.broadcasted_iota(jnp.int32, (8, width), 0)
    query_mask = jnp.logical_and(unit_mask(8, width, 0), row < heads)
    value_mask = jnp.logical_and(unit_mask(8, width, 2 * third - heads * HD), row >= heads)
    take(jnp.logical_or(query_mask, value_mask), qkv_ref[...].reshape(1, width), 0)
    width = fc_ref.shape[0]
    values = fc_ref[...].reshape(1, width)
    take(unit_mask(8, width, 0), values, 128)
    take(unit_mask(8, width, 8 * HD), values, 256)


def pack_sums(flag, vectors, sum_qkv, sum_fc):
    whole = pl.BlockSpec(memory_space=pltpu.VMEM)
    shape = jax.ShapeDtypeStruct((16, vectors[0].shape[0] // 2), jnp.float32)
    return pl.pallas_call(
        pack_sums_kernel,
        in_specs=[pl.BlockSpec(memory_space=pltpu.SMEM)] + [whole] * 8,
        out_shape=[shape, shape],
        name="pack_sums",
    )(flag, *vectors, sum_qkv, sum_fc)


def unpack_sums_kernel(sums_ref, *refs):
    vectors, qv_ref, fc_ref = refs[:6], *refs[6:]
    for row, vector in enumerate(vectors):
        vector[...] = sums_ref[row, :]
    heads, part = qv_ref.shape[1:]
    for which in range(2):
        qv_ref[which] = sums_ref[8 + which * heads : 8 + (which + 1) * heads, :part]
        fc_ref[8 * which : 8 * which + 8, :] = sums_ref[
            8:16, 128 * (which + 1) : 128 * (which + 1) + part
        ]


def unpack_sums(sums, qv_shape, fc_shape):
    vector = jax.ShapeDtypeStruct((sums.shape[1],), jnp.float32)
    return pl.pallas_call(
        unpack_sums_kernel,
        out_shape=[vector] * 6
        + [jax.ShapeDtypeStruct(qv_shape, jnp.float32), jax.ShapeDtypeStruct(fc_shape, jnp.float32)],
        name="unpack_sums",
    )(sums)


def spread_parts(values):
    mate = lax.ppermute(values, "tp", MATE)
    peer = lax.ppermute(values, "tp", PEER)
    across = lax.ppermute(peer, "tp", MATE)
    return (values, mate, peer, across)


def gather_sum(part_of):
    across = lax.ppermute(bf(part_of(3)), "tp", MATE)
    peer = lax.ppermute(bf(part_of(2) + f32(across)), "tp", PEER)
    mate = lax.ppermute(bf(part_of(1)), "tp", MATE)
    return part_of(0) + f32(mate) + f32(peer)


def join_rows(parts):
    return lax.optimization_barrier(jnp.concatenate(parts, axis=0))


def sum_halves(half_of):
    sent = bf(half_of(1))
    other = lax.ppermute(sent, "fsdp", SWAP)
    return bf(half_of(0) + f32(other))


def sum_chained(half_of):
    half = sum_halves(half_of)
    edge = lax.ppermute(half, "ctx", INWARD)
    pair = bf(f32(half) + f32(edge))
    middle = lax.ppermute(pair, "ctx", MIDDLE)
    total = bf(f32(pair) + f32(middle))
    outer = lax.ppermute(total, "ctx", OUTWARD)
    place = lax.axis_index("ctx")
    inner = jnp.logical_and(place > 0, place < 3)
    return f32(jnp.where(inner, total, outer))


def fast_device(
    inputs,
    cotangent,
    ln1_gain,
    ln1_bias,
    qkv_weight,
    qv_bias,
    proj_weight,
    proj_bias,
    ln2_gain,
    ln2_bias,
    fc_weight,
    fc_bias,
    fc2_weight,
    fc2_bias,
):
    row_count, _, width = inputs.shape
    tp_count = lax.axis_size("tp")
    ctx_count = lax.axis_size("ctx")
    share_rows = row_count // tp_count
    share_tokens = share_rows * ctx_count
    place_f = lax.axis_index("fsdp")
    place_c = lax.axis_index("ctx")
    place_t = lax.axis_index("tp")
    place = place_c.astype(jnp.int32).reshape(1)
    half = width // 2
    lower = place_f == 0

    def own_first(values):
        flipped = jnp.concatenate([values[..., half:], values[..., :half]], axis=-1)
        return jnp.where(lower, values, flipped)

    def to_sequences(values):
        mine = lax.dynamic_slice_in_dim(values, place_t * share_rows, share_rows, 0)
        mine = own_first(mine)
        got = []
        for step in range(ctx_count):
            piece = lax.dynamic_index_in_dim(mine, place_c ^ step, 1, keepdims=False)
            if step:
                piece = lax.ppermute(piece, "ctx", xor_pairs(ctx_count, step))
            got.append(piece)
        return jnp.concatenate(got, axis=0)

    def to_positions(values):
        mine = own_first(values)
        got = []
        for step in range(ctx_count):
            piece = mine[step * share_rows : (step + 1) * share_rows]
            if step:
                piece = lax.ppermute(piece, "ctx", xor_pairs(ctx_count, step))
            got.append(piece)
        stacked = jnp.stack(got)
        ordered = [
            lax.dynamic_index_in_dim(stacked, place_c ^ step, 0, keepdims=False)
            for step in range(ctx_count)
        ]
        return jnp.stack(ordered, axis=1)

    flat = f32(to_sequences(inputs))

    flag = place_f.astype(jnp.int32).reshape(1)
    small_own = pack_params(
        (ln1_gain, ln1_bias, proj_bias, ln2_gain, ln2_bias, fc2_bias), qv_bias, fc_bias
    )
    small_other = lax.ppermute(small_own, "fsdp", SWAP)
    qkv_other = lax.ppermute(qkv_weight, "fsdp", SWAP)
    proj_other = lax.ppermute(proj_weight, "fsdp", SWAP)
    fc_other = lax.ppermute(fc_weight, "fsdp", SWAP)
    fc2_other = lax.ppermute(fc2_weight, "fsdp", SWAP)
    proj_full = jnp.concatenate([proj_weight, proj_other], axis=1)
    fc_weight, fc2_weight, fc2_other = lax.optimization_barrier((fc_weight, fc2_weight, fc2_other))
    fc_full = jnp.concatenate([fc_weight, fc_other], axis=0)
    fc2_full = jnp.concatenate([fc2_weight, fc2_other], axis=1)
    qkv_full = jnp.concatenate(
        [
            jnp.concatenate([entry[index] for index in range(3)], axis=1)
            for entry in (qkv_weight, qkv_other)
        ],
        axis=0,
    )

    head_width = qkv_weight.shape[2]
    gain_one, shift_one, bias_proj, gain_two, shift_two, bias_fc2, bias_qkv, bias_row = (
        unpack_params(flag, small_own, small_other, 3 * head_width, fc_weight.shape[1])
    )

    first_f, normed_one, spread_one = norm_forward(flat, gain_one, shift_one)
    first_in = join_rows(spread_parts(bf(first_f)))
    head_shape = (tp_count, ctx_count, share_rows, head_width)
    qkv = bf(matmul(first_in, qkv_full) + bias_qkv)
    qkv = qkv.reshape(head_shape[:3] + (3 * head_width,))
    attended_four, lse = attend(place, qkv)
    attended = attended_four.reshape(-1, head_width)

    def rows_of(values, slot):
        return values[slot * share_tokens : (slot + 1) * share_tokens]

    attn_sum = gather_sum(lambda slot: matmul(rows_of(attended, slot), proj_full))
    mixed = flat + attn_sum + bias_proj
    second_f, normed_two, spread_two = norm_forward(mixed, gain_two, shift_two)
    second_in = spread_parts(bf(second_f))

    grad_own = to_sequences(cotangent)
    grad_rows = spread_parts(grad_own)
    grad_y = f32(grad_own)

    hidden = []
    pre_grad = []
    for slot in range(tp_count):
        hidden_grad = contract(grad_rows[slot], fc2_full, 1, 1)
        pre_act = matmul(second_in[slot], fc_full) + bias_row
        activated, gelu_pull = jax.vjp(partial(jax.nn.gelu, approximate=True), pre_act)
        hidden.append(bf(activated))
        pre_grad.append(bf(gelu_pull(hidden_grad)[0]))

    second_grad = gather_sum(lambda slot: contract(pre_grad[slot], fc_full, 1, 1))
    mixed_grad = grad_y + norm_backward(second_grad, normed_two, spread_two, gain_two)
    branch_own = bf(mixed_grad)
    branch = spread_parts(branch_own)

    mlp_sum = gather_sum(lambda slot: matmul(hidden[slot], fc2_full))
    output = to_positions(bf(mixed + mlp_sum + bias_fc2))

    def halved(values, which):
        return values[:, which * half : (which + 1) * half]

    hidden_all = join_rows(hidden)
    pre_grad_all = join_rows(pre_grad)
    second_all = join_rows(second_in)
    grad_all = join_rows(grad_rows)
    grad_fc2 = sum_chained(lambda which: contract(hidden_all, halved(grad_all, which), 0, 0))
    grad_fc = sum_chained(lambda which: contract(halved(second_all, which), pre_grad_all, 0, 0))

    branch = join_rows(branch)
    attended_grad = bf(contract(branch, proj_full, 1, 1)).reshape(head_shape)
    qkv_grad = attend_back(place, qkv, attended_four, attended_grad, lse).reshape(-1, 3 * head_width)
    grad_proj = sum_chained(lambda which: contract(attended, halved(branch, which), 0, 0))
    grad_qkv = sum_chained(lambda which: contract(halved(first_in, which), qkv_grad, 0, 0))
    grad_qkv = jnp.stack(
        [grad_qkv[:, index * head_width : (index + 1) * head_width] for index in range(3)]
    )

    first_grad = gather_sum(lambda slot: contract(rows_of(qkv_grad, slot), qkv_full, 1, 1))
    input_own = mixed_grad + norm_backward(first_grad, normed_one, spread_one, gain_one)
    input_grad = to_positions(bf(input_own))

    token_sums = (
        jnp.sum(first_grad * normed_one, axis=0),
        jnp.sum(first_grad, axis=0),
        jnp.sum(f32(branch_own), axis=0),
        jnp.sum(second_grad * normed_two, axis=0),
        jnp.sum(second_grad, axis=0),
        jnp.sum(grad_y, axis=0),
    )
    sum_qkv = jnp.sum(f32(qkv_grad), axis=0)
    sum_fc = sum(jnp.sum(f32(part), axis=0) for part in pre_grad)
    kept, sent = pack_sums(flag, token_sums, sum_qkv, sum_fc)
    small = kept + lax.ppermute(sent, "fsdp", SWAP)
    shared = small[:8]
    shared = shared + lax.ppermute(shared, "tp", MATE)
    shared = shared + lax.ppermute(shared, "tp", PEER)
    small = jnp.concatenate([shared, small[8:]], axis=0)
    small = small + lax.ppermute(small, "ctx", xor_pairs(ctx_count, 1))
    small = small + lax.ppermute(small, "ctx", xor_pairs(ctx_count, 2))
    sums = unpack_sums(small, qv_bias.shape, fc_bias.shape)
    return (
        output,
        input_grad,
        sums[0],
        sums[1],
        grad_qkv,
        sums[6],
        grad_proj,
        sums[2],
        sums[3],
        sums[4],
        grad_fc,
        sums[7],
        grad_fc2,
        sums[5],
    )


def on_device(*args):
    rows, sequences, _ = args[0].shape
    whole_sequences = (
        lax.axis_size("fsdp") == 2
        and lax.axis_size("tp") == 4
        and lax.axis_size("ctx") == 4
        and sequences == 4
        and rows == BLOCK
    )
    if not whole_sequences:
        return general_device(*args)
    return fast_device(*args)


def solution(mesh):
    return jax.shard_map(
        on_device,
        mesh=mesh,
        in_specs=(
            P("ctx", "fsdp", None),
            P("ctx", "fsdp", None),
            P("fsdp"),
            P("fsdp"),
            P(None, "fsdp", "tp"),
            P(None, "tp", "fsdp"),
            P("tp", "fsdp"),
            P("fsdp"),
            P("fsdp"),
            P("fsdp"),
            P("fsdp", "tp"),
            P("tp", "fsdp"),
            P("tp", "fsdp"),
            P("fsdp"),
        ),
        out_specs=(
            P(("ctx", "tp"), "fsdp", None),
            P(("ctx", "tp"), "fsdp", None),
            P("fsdp"),
            P("fsdp"),
            P(None, "fsdp", "tp"),
            P(None, "tp", "fsdp"),
            P("tp", "fsdp"),
            P("fsdp"),
            P("fsdp"),
            P("fsdp"),
            P("fsdp", "tp"),
            P("tp", "fsdp"),
            P("tp", "fsdp"),
            P("fsdp"),
        ),
        check_vma=False,
    )
```
